32 devices in a mesh: row: 2 (over y), col: 16 (over z, x, core).
Axes of the slice: x: 2, y: 2, z: 4, core: 2. Of those that a mesh axis runs over, the one named last changes fastest.
Arguments:
- a_blocks: bfloat16 [2, 16, 320, 64, 64], P('row', 'col'), may hold values from -1.25 to 1.25
- block_rows: int32 [2, 16, 320], P('row', 'col'), may hold values from 0 to 255
- block_cols: int32 [2, 16, 320], P('row', 'col'), may hold values from 0 to 31
- block_count: int32 [2, 16], P('row', 'col'), may hold values from 160 to 320, as said below
- restrict: bfloat16 [512, 64, 64], P(('row', 'col')), may hold values from -0.75 to 0.75
- interp: bfloat16 [512, 64, 64], P('col', 'row'), may hold values from -0.75 to 0.75
- aggregate: int32 [512], replicated, may hold values from 0 to 15, as said below
- owner: int32 [16], replicated, may hold values from 0 to 15, each once
Outputs:
- coarse: float32 [16, 16, 64, 64], P('col')
The draws below stay inside these ranges and needn't reach their ends.
Inputs may be any that keep to these rules, and one draw needn't show every extreme that they name: `block_count`: at least one device holds 320 live blocks in every draw. aggregate[i] differs from i * 16 // 512 by at most one, and by exactly one for some block in every draw.
All inputs are finite; a program needn't handle non-finite values.
Results may differ from the reference program's by a relative error of at most 0.0029.
Values may be sent and summed in bfloat16 or wider, within the bound.
A program may use at most 128 MiB of HBM per device.

```python
import jax
import jax.numpy as jnp
from jax import lax

BS = 64
RB = 256
NNZ_DEV = 320
NFB = 512
CB = 32
NA = 16
N_ROW = 2
N_COL = 16


def draw_block_count(key, part):
    first, second = jax.random.split(key)
    counts = jax.random.randint(first, (N_ROW * N_COL,), NNZ_DEV // 2, NNZ_DEV + 1)
    fullest = jax.random.randint(second, (), 0, N_ROW * N_COL)
    counts = jnp.where(jnp.arange(N_ROW * N_COL) == fullest, NNZ_DEV, counts)
    return counts.reshape(N_ROW, N_COL).astype(jnp.int32)


def draw_aggregate(key, part):
    coins = jax.random.randint(jax.random.fold_in(key, 17), (NFB,), 0, 2)
    index = jnp.arange(NFB, dtype=jnp.int32)
    per_agg = NFB // NA
    base = index // per_agg
    place = index % per_agg
    shift = jnp.where((place == 0) & (coins == 1), -1, 0)
    shift = jnp.where((place == per_agg - 1) & (coins == 1), 1, shift)
    shift = jnp.where(index == per_agg, -1, shift)
    return jnp.clip(base + shift, 0, NA - 1).astype(jnp.int32)


def plant(values, own_key, smallest, top_value):
    extent = values.shape
    spot = [jax.random.randint(jax.random.fold_in(own_key, axis), (), 0, extent[axis]) for axis in range(len(extent))]
    values = values.at[tuple(spot)].set(smallest)
    longest = extent.index(max(extent))
    spot[longest] = (spot[longest] + 1) % extent[longest]
    return values.at[tuple(spot)].set(top_value)


def shard_levels(own_key, dims, cuts, least, top_value):
    def one(dim, parts):
        steps = jax.random.uniform(jax.random.fold_in(jax.random.fold_in(own_key, 6), dim), (parts,), jnp.float32, least / len(cuts), top_value / len(cuts))
        return jnp.repeat(jnp.exp(steps), dims[dim] // parts).reshape((-1,) + (1,) * (len(dims) - dim - 1))

    level = one(*cuts[0])
    for cut in cuts[1:]:
        level = level * one(*cut)
    return level


def gaussian(own_key, dims, scale, reach, pieces=(), held_as=jnp.bfloat16):
    level = shard_levels(own_key, dims, pieces, -0.22, 0.18) if pieces else 1.0
    drawn = jax.random.normal(own_key, dims, jnp.float32) * scale * level
    return jnp.minimum(jnp.maximum(drawn, -reach), reach).astype(held_as)


def setup_inputs(seed: int = 0) -> dict:
    keys = jax.random.split(jax.random.key(seed), 9)
    return {
        "a_blocks": gaussian(keys[0], (N_ROW, N_COL, NNZ_DEV, BS, BS), (0.64 / BS ** 0.5), 1.25, ((0, 2), (1, 16))),
        "block_rows": plant(jax.random.randint(keys[1], (N_ROW, N_COL, NNZ_DEV), 0, RB), jax.random.fold_in(keys[1], 1), 0, RB - 1).astype(jnp.int32),
        "block_cols": plant(jax.random.randint(keys[2], (N_ROW, N_COL, NNZ_DEV), 0, CB), jax.random.fold_in(keys[2], 1), 0, CB - 1).astype(jnp.int32),
        "block_count": draw_block_count(jax.random.fold_in(keys[8], 71), 0),
        "restrict": gaussian(keys[4], (NFB, BS, BS), BS ** -0.5, 0.75, ((0, 32),)),
        "interp": gaussian(keys[5], (NFB, BS, BS), BS ** -0.5, 0.75, ((0, 16), (1, 2))),
        "aggregate": draw_aggregate(jax.random.fold_in(keys[8], 71), 0),
        "owner": jax.random.permutation(keys[7], NA).astype(jnp.int32),
    }


def reference(a_blocks, block_rows, block_cols, block_count, restrict, interp, aggregate, owner):
    flat_blocks = a_blocks.reshape(N_ROW * N_COL, NNZ_DEV, BS, BS)
    flat_rows = block_rows.reshape(N_ROW * N_COL, NNZ_DEV)
    flat_cols = block_cols.reshape(N_ROW * N_COL, NNZ_DEV)
    flat_count = block_count.reshape(N_ROW * N_COL)
    device_ids = jnp.arange(N_ROW * N_COL, dtype=jnp.int32)

    def one_device(total, items):
        blocks, rows, cols, count, device = items
        row_index = device // N_COL
        col_index = device % N_COL
        fine_rows = row_index * RB + rows
        fine_cols = col_index * CB + cols
        product = jnp.einsum("pxy,pyz->pxz", blocks.astype(jnp.float32), interp[fine_cols].astype(jnp.float32)).astype(jnp.bfloat16)
        term = jnp.einsum("pxy,pyz->pxz", restrict[fine_rows].astype(jnp.float32), product.astype(jnp.float32))
        live = (jnp.arange(NNZ_DEV, dtype=jnp.int32) < count).astype(jnp.float32)
        term = term * live[:, None, None]
        pair_ids = owner[aggregate[fine_rows]] * NA + aggregate[fine_cols]
        summed = jax.ops.segment_sum(term.reshape(NNZ_DEV, BS * BS), pair_ids, NA * NA)
        return total + summed, None

    start = jnp.zeros((NA * NA, BS * BS), jnp.float32)
    total, _ = lax.scan(one_device, start, (flat_blocks, flat_rows, flat_cols, flat_count, device_ids))
    return total.reshape(NA, NA, BS, BS)
```

```python
import functools

import jax
import jax.numpy as jnp
from jax import lax
from jax.experimental import pallas as pl
from jax.experimental.pallas import tpu as pltpu
from jax.sharding import PartitionSpec as P

MESH = pl.DeviceIdType.MESH
CORES = 2
DEPTH = 4


def gather_kernel(n_row, n_col, r_ref, p_ref, rg_ref, pg_ref, send_sem, recv_sem, psend_sem, precv_sem):
    width = n_col // (CORES * DEPTH)
    me = lax.axis_index("col")
    row = lax.axis_index("row")
    z = me // (width * CORES)
    x = lax.rem(me // CORES, width)
    k = lax.rem(me, CORES)
    sibling = me + 1 - 2 * k
    hop = width * CORES
    other_x = [(z * width + lax.rem(x + d, width)) * CORES + k for d in range(1, width)]
    other_row = [lax.rem(row + d, n_row) for d in range(1, n_row)]

    barrier = pltpu.get_barrier_semaphore()

    def greet(dev):
        pl.semaphore_signal(barrier, inc=1, device_id=dev, device_id_type=MESH)

    for o in other_row:
        greet((o, me))
    greet((row, sibling))
    for o in other_x:
        greet((row, o))

    @pl.when(z > 0)
    def _():
        greet((row, me - hop))

    @pl.when(z < DEPTH - 1)
    def _():
        greet((row, me + hop))

    half_r = r_ref.shape[0] // 2
    for i in range(half_r):
        rg_ref[me, i, :, 0:64] = r_ref[i]
        rg_ref[me, i, :, 64:128] = r_ref[i + half_r]
    half_p = p_ref.shape[0] // 2
    for j in range(half_p):
        pg_ref[row, j, :, 0:64] = p_ref[j]
        pg_ref[row, j, :, 64:128] = p_ref[j + half_p]

    fixed = len(other_row) + 1 + len(other_x)
    pl.semaphore_wait(barrier, fixed + jnp.where(z > 0, 1, 0) + jnp.where(z < DEPTH - 1, 1, 0))

    def rcopy(shard, way, target):
        return pltpu.make_async_remote_copy(
            src_ref=rg_ref.at[shard],
            dst_ref=rg_ref.at[shard],
            send_sem=send_sem.at[shard, way],
            recv_sem=recv_sem.at[shard],
            device_id=(row, target),
            device_id_type=MESH,
        )

    def pcopy(way, target):
        return pltpu.make_async_remote_copy(
            src_ref=pg_ref.at[row],
            dst_ref=pg_ref.at[row],
            send_sem=psend_sem.at[way],
            recv_sem=precv_sem.at[row],
            device_id=(target, me),
            device_id_type=MESH,
        )

    @pl.when(z > 0)
    def _():
        rcopy(me, 1, me - hop).start()

    @pl.when(z < DEPTH - 1)
    def _():
        rcopy(me, 2, me + hop).start()

    def spread(shard):
        for w, o in enumerate(other_x):
            rcopy(shard, 3 + w, o).start()
        rcopy(shard, 0, sibling).start()

    spread(me)
    for w, o in enumerate(other_row):
        pcopy(w, o).start()

    def from_x(d):
        for sign in ((1,) if d == 0 else (-1, 1)):
            @pl.when((z + sign * d >= 0) & (z + sign * d < DEPTH))
            def _():
                for o in other_x:
                    shard = o + sign * d * hop
                    rcopy(shard, 0, sibling).wait_recv()
                    rcopy(shard, 0, sibling).start()

    for d in range(1, DEPTH):
        @pl.when(z - d >= 0)
        def _():
            shard = me - d * hop
            rcopy(shard, 0, sibling).wait_recv()

            @pl.when(z < DEPTH - 1)
            def _():
                rcopy(shard, 2, me + hop).start()

            spread(shard)

        @pl.when(z + d < DEPTH)
        def _():
            shard = me + d * hop
            rcopy(shard, 0, sibling).wait_recv()

            @pl.when(z > 0)
            def _():
                rcopy(shard, 1, me - hop).start()

            spread(shard)

        from_x(d - 1)
    from_x(DEPTH - 1)

    for other in range(n_col // CORES):
        shard = other * CORES + 1 - k
        rcopy(shard, 0, sibling).wait_recv()
    for o in other_row:
        pltpu.make_async_remote_copy(
            src_ref=pg_ref.at[o], dst_ref=pg_ref.at[o], send_sem=psend_sem.at[0], recv_sem=precv_sem.at[o],
            device_id=(o, me), device_id_type=MESH,
        ).wait_recv()
    for other in range(n_col // CORES):
        rcopy(other * CORES + k, 0, sibling).wait_send()
    for zz in range(DEPTH):
        shard = (zz * width + x) * CORES + k
        for w in range(len(other_x)):
            rcopy(shard, 3 + w, me).wait_send()

        @pl.when((z > 0) & (zz >= z))
        def _():
            rcopy(shard, 1, me).wait_send()

        @pl.when((z < DEPTH - 1) & (zz <= z))
        def _():
            rcopy(shard, 2, me).wait_send()
    for w in range(len(other_row)):
        pcopy(w, row).wait_send()


def compute_kernel(n_row, n_col, row_width, col_width, unroll, rows_ref, cols_ref, count_ref, agg_ref, a_ref, pg_ref, rg_ref, out_ref, p_full, r_full, acc):
    row = lax.axis_index("row")
    col = lax.axis_index("col")
    half_p = pg_ref.shape[1]
    piece = pg_ref.shape[2]
    half_r = rg_ref.shape[1]
    panel_rows = n_col * 2 * half_r
    panel_cols = 2 * half_p
    n_seg = row_width * col_width
    agg_total = n_col
    row_base = row * (agg_total // n_row) - 1
    col_base = col - 1

    acc[...] = jnp.zeros_like(acc)

    def unpack_p(j, _):
        for r in range(n_row):
            both = pg_ref[r, j]
            p_full[j, r * piece:(r + 1) * piece, :] = both[:, 0:64]
            p_full[j + half_p, r * piece:(r + 1) * piece, :] = both[:, 64:128]
        return 0

    lax.fori_loop(0, half_p, unpack_p, 0, unroll=4)

    def unpack_r(c, _):
        for i in range(half_r):
            both = rg_ref[c, i]
            r_full[c * 2 * half_r + i] = both[:, 0:64]
            r_full[c * 2 * half_r + half_r + i] = both[:, 64:128]
        return 0

    lax.fori_loop(0, n_col, unpack_r, 0)

    count = count_ref[0, 0]

    def group(g, _):
        base = g * unroll
        prods = []
        for u in range(unroll):
            prods.append(
                jnp.dot(a_ref[base + u], p_full[cols_ref[0, base + u]], preferred_element_type=jnp.float32).astype(jnp.bfloat16)
            )
        terms = [
            jnp.dot(r_full[rows_ref[0, base + u]], prods[u], preferred_element_type=jnp.float32) for u in range(unroll)
        ]
        for u in range(unroll):
            p = base + u
            ra = agg_ref[row * panel_rows + rows_ref[0, p]] - row_base
            ca = agg_ref[col * panel_cols + cols_ref[0, p]] - col_base
            seg = jnp.where(p < count, ra * col_width + ca, n_seg)
            acc[seg] += terms[u]
        return 0

    lax.fori_loop(0, pl.cdiv(count, unroll), group, 0)
    for ca in range(col_width):
        for ra in range(row_width):
            block = acc[ra * col_width + ca]
            out_ref[ca, ra, :, 0:64] = block[0:32]
            out_ref[ca, ra, :, 64:128] = block[32:64]


def reduce_kernel(n_row, n_col, row_width, owner_ref, part_ref, out_ref, edge, total, outgoing, incoming, esend_sem, erecv_sem, send_sem, recv_sem):
    row = lax.axis_index("row")
    col = lax.axis_index("col")
    n_dev = n_row * n_col
    me = row * n_col + col
    row_base = row * (n_col // n_row) - 1

    barrier = pltpu.get_barrier_semaphore()

    def greet(i, _):
        dev = lax.rem(me + i, n_dev)
        pl.semaphore_signal(barrier, inc=1, device_id=(dev // n_col, lax.rem(dev, n_col)), device_id_type=MESH)
        return 0

    lax.fori_loop(1, n_dev, greet, 0)
    pl.semaphore_wait(barrier, n_dev - 1)

    def ecopy(slot, side, target):
        return pltpu.make_async_remote_copy(
            src_ref=part_ref.at[slot], dst_ref=edge.at[side], send_sem=esend_sem.at[side], recv_sem=erecv_sem.at[side],
            device_id=(row, target), device_id_type=MESH,
        )

    down = ecopy(0, 1, col - 1)
    up = ecopy(2, 0, col + 1)

    @pl.when(col > 0)
    def _():
        down.start()

    @pl.when(col < n_col - 1)
    def _():
        up.start()

    total[...] = part_ref[1]

    @pl.when(col > 0)
    def _():
        up.wait_recv()
        total[...] += edge[0]

    @pl.when(col < n_col - 1)
    def _():
        down.wait_recv()
        total[...] += edge[1]

    def dcopy(dev):
        return pltpu.make_async_remote_copy(
            src_ref=outgoing.at[lax.rem(dev, n_col)], dst_ref=incoming.at[me], send_sem=send_sem.at[dev], recv_sem=recv_sem.at[me],
            device_id=(dev // n_col, lax.rem(dev, n_col)), device_id_type=MESH,
        )

    def post(i, _):
        s = lax.rem(col + i, n_col)
        a = lax.fori_loop(0, n_col, lambda t, got: jnp.where(owner_ref[t] == s, t, got), 0, unroll=True)
        idx = a - row_base
        valid = (idx >= 0) & (idx < row_width)
        block = total[jnp.clip(idx, 0, row_width - 1)]
        outgoing[s] = jnp.where(valid, block, 0.0).astype(jnp.bfloat16)
        for rr in range(n_row):
            dev = rr * n_col + s

            @pl.when(dev != me)
            def _():
                dcopy(dev).start()
        return 0

    lax.fori_loop(0, n_col, post, 0)
    incoming[me] = outgoing[col]

    def arrive(i, _):
        dev = lax.rem(me + i, n_dev)
        pltpu.make_async_remote_copy(
            src_ref=outgoing.at[0], dst_ref=incoming.at[dev], send_sem=send_sem.at[dev], recv_sem=recv_sem.at[dev],
            device_id=(dev // n_col, lax.rem(dev, n_col)), device_id_type=MESH,
        ).wait_recv()
        return 0

    lax.fori_loop(1, n_dev, arrive, 0)

    def emit(c, _):
        block = incoming[c].astype(jnp.float32)
        for rr in range(1, n_row):
            block += incoming[rr * n_col + c].astype(jnp.float32)
        out_ref[0, c, 0:32, :] = block[:, 0:64]
        out_ref[0, c, 32:64, :] = block[:, 64:128]
        return 0

    lax.fori_loop(0, n_col, emit, 0)

    def sent(i, _):
        dcopy(lax.rem(me + i, n_dev)).wait_send()
        return 0

    lax.fori_loop(1, n_dev, sent, 0)

    @pl.when(col > 0)
    def _():
        down.wait_send()

    @pl.when(col < n_col - 1)
    def _():
        up.wait_send()


def on_device(n_row, n_col, a_blocks, block_rows, block_cols, block_count, restrict, interp, aggregate, owner):
    vmem = pl.BlockSpec(memory_space=pltpu.VMEM)
    smem = pl.BlockSpec(memory_space=pltpu.SMEM)
    width = n_col // (CORES * DEPTH)
    nb = restrict.shape[0]
    nj, piece = interp.shape[:2]
    slots = a_blocks.shape[2]
    agg_total = owner.shape[0]
    assert agg_total == n_col
    row_width = agg_total // n_row + 2
    col_width = 3
    limit = 48 * 2**20
    rg, pg = pl.pallas_call(
        functools.partial(gather_kernel, n_row, n_col),
        out_shape=(
            jax.ShapeDtypeStruct((n_col, nb // 2, 64, 128), jnp.bfloat16),
            jax.ShapeDtypeStruct((n_row, nj // 2, piece, 128), jnp.bfloat16),
        ),
        in_specs=[vmem, vmem],
        out_specs=(vmem, vmem),
        scratch_shapes=[
            pltpu.SemaphoreType.DMA((n_col, 3 + width)),
            pltpu.SemaphoreType.DMA((n_col,)),
            pltpu.SemaphoreType.DMA((n_row,)),
            pltpu.SemaphoreType.DMA((n_row,)),
        ],
        compiler_params=pltpu.CompilerParams(collective_id=0, has_side_effects=True, vmem_limit_bytes=limit),
        name="gather_panels",
    )(restrict, interp)
    part = pl.pallas_call(
        functools.partial(compute_kernel, n_row, n_col, row_width, col_width, 8),
        out_shape=jax.ShapeDtypeStruct((col_width, row_width, 32, 128), jnp.float32),
        in_specs=[smem, smem, smem, smem, vmem, vmem, vmem],
        out_specs=vmem,
        scratch_shapes=[
            pltpu.VMEM((nj, 64, 64), jnp.bfloat16),
            pltpu.VMEM((n_col * nb, 64, 64), jnp.bfloat16),
            pltpu.VMEM((row_width * col_width + 1, 64, 64), jnp.float32),
        ],
        compiler_params=pltpu.CompilerParams(vmem_limit_bytes=limit),
        name="local_terms",
    )(block_rows[0], block_cols[0], block_count, aggregate, a_blocks[0, 0], pg, rg)
    n_dev = n_row * n_col
    return pl.pallas_call(
        functools.partial(reduce_kernel, n_row, n_col, row_width),
        out_shape=jax.ShapeDtypeStruct((1, agg_total, 64, 64), jnp.float32),
        in_specs=[smem, vmem],
        out_specs=vmem,
        scratch_shapes=[
            pltpu.VMEM((2, row_width, 32, 128), jnp.float32),
            pltpu.VMEM((row_width, 32, 128), jnp.float32),
            pltpu.VMEM((n_col, 32, 128), jnp.bfloat16),
            pltpu.VMEM((n_dev, 32, 128), jnp.bfloat16),
            pltpu.SemaphoreType.DMA((2,)),
            pltpu.SemaphoreType.DMA((2,)),
            pltpu.SemaphoreType.DMA((n_dev,)),
            pltpu.SemaphoreType.DMA((n_dev,)),
        ],
        compiler_params=pltpu.CompilerParams(collective_id=1, has_side_effects=True, vmem_limit_bytes=limit),
        name="reduce_coarse",
    )(owner, part)


def solution(mesh):
    return jax.shard_map(
        functools.partial(on_device, mesh.shape["row"], mesh.shape["col"]),
        mesh=mesh,
        in_specs=(
            P("row", "col", None, None, None),
            P("row", "col", None),
            P("row", "col", None),
            P("row", "col"),
            P(("row", "col"), None, None),
            P("col", "row", None),
            P(),
            P(),
        ),
        out_specs=P("col", None, None, None),
        check_vma=False,
    )
```

```python
import functools

import jax
import jax.numpy as jnp
from jax import lax
from jax.experimental import pallas as pl
from jax.experimental.pallas import tpu as pltpu
from jax.sharding import PartitionSpec as P

MESH = pl.DeviceIdType.MESH
CORES = 2
DEPTH = 4


def gather_kernel(n_row, n_col, unroll, cols_ref, r_hbm, p_hbm, a_hbm, r_full, prod_ref, r_ref, p_ref, a_ref, rg_ref, pg_ref, flat, wide, load_sem, send_sem, recv_sem, psend_sem, precv_sem):
    width = n_col // (CORES * DEPTH)
    me = lax.axis_index("col")
    row = lax.axis_index("row")
    z = me // (width * CORES)
    x = lax.rem(me // CORES, width)
    k = lax.rem(me, CORES)
    sibling = me + 1 - 2 * k
    hop = width * CORES
    other_x = [(z * width + lax.rem(x + d, width)) * CORES + k for d in range(1, width)]
    other_row = [lax.rem(row + d, n_row) for d in range(1, n_row)]
    nb = r_ref.shape[0]
    half_r = nb // 2
    half_p = p_ref.shape[0] // 2
    piece = p_ref.shape[1]
    slots = a_ref.shape[2]

    load_r = pltpu.make_async_copy(r_hbm, r_ref, load_sem.at[0])
    load_p = pltpu.make_async_copy(p_hbm, p_ref, load_sem.at[1])
    load_a = pltpu.make_async_copy(a_hbm, a_ref, load_sem.at[2])
    load_r.start()
    load_p.start()
    load_a.start()

    barrier = pltpu.get_barrier_semaphore()

    def greet(dev):
        pl.semaphore_signal(barrier, inc=1, device_id=dev, device_id_type=MESH)

    for o in other_row:
        greet((o, me))
    greet((row, sibling))
    for o in other_x:
        greet((row, o))

    @pl.when(z > 0)
    def _():
        greet((row, me - hop))

    @pl.when(z < DEPTH - 1)
    def _():
        greet((row, me + hop))

    load_r.wait()
    for i in range(half_r):
        rg_ref[me, i, :, 0:64] = r_ref[i]
        rg_ref[me, i, :, 64:128] = r_ref[i + half_r]
    load_p.wait()
    for j in range(half_p):
        pg_ref[row, j, :, 0:64] = p_ref[j]
        pg_ref[row, j, :, 64:128] = p_ref[j + half_p]

    fixed = len(other_row) + 1 + len(other_x)
    pl.semaphore_wait(barrier, fixed + jnp.where(z > 0, 1, 0) + jnp.where(z < DEPTH - 1, 1, 0))

    def rcopy(shard, way, target):
        return pltpu.make_async_remote_copy(
            src_ref=rg_ref.at[shard],
            dst_ref=rg_ref.at[shard],
            send_sem=send_sem.at[shard, way],
            recv_sem=recv_sem.at[shard],
            device_id=(row, target),
            device_id_type=MESH,
        )

    def pcopy(way, target):
        return pltpu.make_async_remote_copy(
            src_ref=pg_ref.at[row],
            dst_ref=pg_ref.at[row],
            send_sem=psend_sem.at[way],
            recv_sem=precv_sem.at[row],
            device_id=(target, me),
            device_id_type=MESH,
        )

    def spread(shard):
        for w, o in enumerate(other_x):
            rcopy(shard, 3 + w, o).start()
        rcopy(shard, 0, sibling).start()

    @pl.when(z > 0)
    def _():
        rcopy(me, 1, me - hop).start()

    @pl.when(z < DEPTH - 1)
    def _():
        rcopy(me, 2, me + hop).start()

    for w, o in enumerate(other_row):
        pcopy(w, o).start()
    spread(me)

    def from_z(d):
        @pl.when(z - d >= 0)
        def _():
            shard = me - d * hop
            rcopy(shard, 0, sibling).wait_recv()

            @pl.when(z < DEPTH - 1)
            def _():
                rcopy(shard, 2, me + hop).start()

            spread(shard)

        @pl.when(z + d < DEPTH)
        def _():
            shard = me + d * hop
            rcopy(shard, 0, sibling).wait_recv()

            @pl.when(z > 0)
            def _():
                rcopy(shard, 1, me - hop).start()

            spread(shard)

    def from_x(d):
        for sign in ((1,) if d == 0 else (-1, 1)):
            @pl.when((z + sign * d >= 0) & (z + sign * d < DEPTH))
            def _():
                for o in other_x:
                    shard = o + sign * d * hop
                    rcopy(shard, 0, sibling).wait_recv()
                    rcopy(shard, 0, sibling).start()

    def turn(lo, hi):
        def body(i, _):
            for s in range(0, slots, 128):
                e = min(s + 128, slots)
                tall = jnp.concatenate([a_ref[i, :, s:e], a_ref[i + 32, :, s:e]], axis=0)
                flat[pl.ds(pl.multiple_of(i * slots + s, 8), e - s), :] = tall.astype(jnp.float32).T
            return 0

        lax.fori_loop(lo, hi, body, 0)

    def multiply(lo, hi):
        def body(g, _):
            base = g * unroll
            for u in range(unroll):
                p = base + u
                left = flat[pl.ds(p, 32, stride=slots), :].astype(jnp.bfloat16)
                prod_ref[p] = jnp.dot(
                    left, wide[cols_ref[0, p]], preferred_element_type=jnp.float32
                ).astype(jnp.bfloat16)
            return 0

        lax.fori_loop(lo, hi, body, 0)

    def widen(j, _):
        for r in range(n_row):
            lo, hi = r * piece, (r + 1) * piece
            both = pg_ref[r, j]
            wide[j, lo:hi, 0:64] = both[:, 0:64]
            wide[j, 64 + lo:64 + hi, 64:128] = both[:, 0:64]
            wide[j + half_p, lo:hi, 0:64] = both[:, 64:128]
            wide[j + half_p, 64 + lo:64 + hi, 64:128] = both[:, 64:128]
        return 0

    load_a.wait()
    turn(0, 12)
    from_z(1)
    turn(12, 22)
    from_x(0)
    turn(22, 32)
    from_z(2)
    for o in other_row:
        pltpu.make_async_remote_copy(
            src_ref=pg_ref.at[o], dst_ref=pg_ref.at[o], send_sem=psend_sem.at[0], recv_sem=precv_sem.at[o],
            device_id=(o, me), device_id_type=MESH,
        ).wait_recv()
    wide[...] = jnp.zeros_like(wide)
    lax.fori_loop(0, half_p, widen, 0, unroll=2)
    from_x(1)
    groups = slots // unroll
    multiply(0, groups // 4)
    from_z(3)
    multiply(groups // 4, groups // 2)
    from_x(2)
    multiply(groups // 2, 3 * groups // 4)
    from_x(3)
    multiply(3 * groups // 4, groups)

    def unpack(shard):
        for i in range(half_r):
            both = rg_ref[shard, i]
            r_full[shard * nb + i] = both[:, 0:64]
            r_full[shard * nb + half_r + i] = both[:, 64:128]

    def unpack_mine(other, _):
        unpack(other * CORES + k)
        return 0

    lax.fori_loop(0, n_col // CORES, unpack_mine, 0)

    def unpack_sibling(other, _):
        shard = other * CORES + 1 - k
        rcopy(shard, 0, sibling).wait_recv()
        unpack(shard)
        return 0

    lax.fori_loop(0, n_col // CORES, unpack_sibling, 0)
    for other in range(n_col // CORES):
        rcopy(other * CORES + k, 0, sibling).wait_send()
    for zz in range(DEPTH):
        shard = (zz * width + x) * CORES + k
        for w in range(len(other_x)):
            rcopy(shard, 3 + w, me).wait_send()

        @pl.when((z > 0) & (zz >= z))
        def _():
            rcopy(shard, 1, me).wait_send()

        @pl.when((z < DEPTH - 1) & (zz <= z))
        def _():
            rcopy(shard, 2, me).wait_send()
    for w in range(len(other_row)):
        pcopy(w, row).wait_send()


def compute_kernel(n_row, n_col, row_width, col_width, unroll, rows_ref, cols_ref, count_ref, agg_ref, prod_ref, r_full, out_ref, acc):
    row = lax.axis_index("row")
    col = lax.axis_index("col")
    panel_rows = r_full.shape[0]
    panel_cols = agg_ref.shape[0] // n_col
    n_seg = row_width * col_width
    agg_total = n_col
    row_base = row * (agg_total // n_row) - 1
    col_base = col - 1

    acc[...] = jnp.zeros_like(acc)
    count = count_ref[0, 0]

    def group(g, _):
        base = g * unroll
        terms = []
        for u in range(unroll):
            both = prod_ref[base + u]
            right = jnp.concatenate([both[:, 0:64], both[:, 64:128]], axis=0)
            terms.append(jnp.dot(r_full[rows_ref[0, base + u]], right, preferred_element_type=jnp.float32))
        for u in range(unroll):
            p = base + u
            ra = agg_ref[row * panel_rows + rows_ref[0, p]] - row_base
            ca = agg_ref[col * panel_cols + cols_ref[0, p]] - col_base
            seg = jnp.where(p < count, ra * col_width + ca, n_seg)
            acc[seg] += terms[u]
        return 0

    lax.fori_loop(0, pl.cdiv(count, unroll), group, 0)
    for ca in range(col_width):
        for ra in range(row_width):
            block = acc[ra * col_width + ca]
            out_ref[ca, ra, :, 0:64] = block[0:32]
            out_ref[ca, ra, :, 64:128] = block[32:64]


def reduce_kernel(n_row, n_col, row_width, owner_ref, part_ref, out_ref, edge, total, outgoing, incoming, esend_sem, erecv_sem, send_sem, recv_sem):
    row = lax.axis_index("row")
    col = lax.axis_index("col")
    n_dev = n_row * n_col
    me = row * n_col + col
    row_base = row * (n_col // n_row) - 1

    barrier = pltpu.get_barrier_semaphore()

    def greet(i, _):
        dev = lax.rem(me + i, n_dev)
        pl.semaphore_signal(barrier, inc=1, device_id=(dev // n_col, lax.rem(dev, n_col)), device_id_type=MESH)
        return 0

    lax.fori_loop(1, n_dev, greet, 0)
    pl.semaphore_wait(barrier, n_dev - 1)

    def ecopy(slot, side, target):
        return pltpu.make_async_remote_copy(
            src_ref=part_ref.at[slot], dst_ref=edge.at[side], send_sem=esend_sem.at[side], recv_sem=erecv_sem.at[side],
            device_id=(row, target), device_id_type=MESH,
        )

    down = ecopy(0, 1, col - 1)
    up = ecopy(2, 0, col + 1)

    @pl.when(col > 0)
    def _():
        down.start()

    @pl.when(col < n_col - 1)
    def _():
        up.start()

    total[...] = part_ref[1]

    @pl.when(col > 0)
    def _():
        up.wait_recv()
        total[...] += edge[0]

    @pl.when(col < n_col - 1)
    def _():
        down.wait_recv()
        total[...] += edge[1]

    def dcopy(dev):
        return pltpu.make_async_remote_copy(
            src_ref=outgoing.at[lax.rem(dev, n_col)], dst_ref=incoming.at[me], send_sem=send_sem.at[dev], recv_sem=recv_sem.at[me],
            device_id=(dev // n_col, lax.rem(dev, n_col)), device_id_type=MESH,
        )

    def post(i, _):
        s = lax.rem(col + i, n_col)
        a = lax.fori_loop(0, n_col, lambda t, got: jnp.where(owner_ref[t] == s, t, got), 0, unroll=True)
        idx = a - row_base
        valid = (idx >= 0) & (idx < row_width)
        block = total[jnp.clip(idx, 0, row_width - 1)]
        outgoing[s] = jnp.where(valid, block, 0.0).astype(jnp.bfloat16)
        for rr in range(n_row):
            dev = rr * n_col + s

            @pl.when(dev != me)
            def _():
                dcopy(dev).start()
        return 0

    lax.fori_loop(0, n_col, post, 0)
    incoming[me] = outgoing[col]

    def arrive(i, _):
        dev = lax.rem(me + i, n_dev)
        pltpu.make_async_remote_copy(
            src_ref=outgoing.at[0], dst_ref=incoming.at[dev], send_sem=send_sem.at[dev], recv_sem=recv_sem.at[dev],
            device_id=(dev // n_col, lax.rem(dev, n_col)), device_id_type=MESH,
        ).wait_recv()
        return 0

    lax.fori_loop(1, n_dev, arrive, 0)

    def emit(c, _):
        block = incoming[c].astype(jnp.float32)
        for rr in range(1, n_row):
            block += incoming[rr * n_col + c].astype(jnp.float32)
        out_ref[0, c, 0:32, :] = block[:, 0:64]
        out_ref[0, c, 32:64, :] = block[:, 64:128]
        return 0

    lax.fori_loop(0, n_col, emit, 0)

    def sent(i, _):
        dcopy(lax.rem(me + i, n_dev)).wait_send()
        return 0

    lax.fori_loop(1, n_dev, sent, 0)

    @pl.when(col > 0)
    def _():
        down.wait_send()

    @pl.when(col < n_col - 1)
    def _():
        up.wait_send()


def on_device(n_row, n_col, a_blocks, block_rows, block_cols, block_count, restrict, interp, aggregate, owner):
    vmem = pl.BlockSpec(memory_space=pltpu.VMEM)
    smem = pl.BlockSpec(memory_space=pltpu.SMEM)
    width = n_col // (CORES * DEPTH)
    nb = restrict.shape[0]
    nj, piece = interp.shape[:2]
    slots = a_blocks.shape[2]
    agg_total = owner.shape[0]
    assert agg_total == n_col
    row_width = agg_total // n_row + 2
    col_width = 3
    limit = 40 * 2**20
    hbm = pl.BlockSpec(memory_space=pltpu.HBM)
    sized = jnp.transpose(a_blocks[0, 0], (1, 2, 0))
    r_full, prod = pl.pallas_call(
        functools.partial(gather_kernel, n_row, n_col, 8),
        out_shape=(
            jax.ShapeDtypeStruct((n_col * nb, 64, 64), jnp.bfloat16),
            jax.ShapeDtypeStruct((slots, 32, 128), jnp.bfloat16),
        ),
        in_specs=[smem, hbm, hbm, hbm],
        out_specs=(vmem, vmem),
        scratch_shapes=[
            pltpu.VMEM((nb, 64, 64), jnp.bfloat16),
            pltpu.VMEM((nj, piece, 64), jnp.bfloat16),
            pltpu.VMEM((64, 64, slots), jnp.bfloat16),
            pltpu.VMEM((n_col, nb // 2, 64, 128), jnp.bfloat16),
            pltpu.VMEM((n_row, nj // 2, piece, 128), jnp.bfloat16),
            pltpu.VMEM((32 * slots, 128), jnp.float32),
            pltpu.VMEM((nj, 128, 128), jnp.bfloat16),
            pltpu.SemaphoreType.DMA((3,)),
            pltpu.SemaphoreType.DMA((n_col, 3 + width)),
            pltpu.SemaphoreType.DMA((n_col,)),
            pltpu.SemaphoreType.DMA((n_row,)),
            pltpu.SemaphoreType.DMA((n_row,)),
        ],
        compiler_params=pltpu.CompilerParams(collective_id=0, has_side_effects=True, vmem_limit_bytes=limit),
        name="gather_panels",
    )(block_cols[0], restrict, interp, sized)
    part = pl.pallas_call(
        functools.partial(compute_kernel, n_row, n_col, row_width, col_width, 8),
        out_shape=jax.ShapeDtypeStruct((col_width, row_width, 32, 128), jnp.float32),
        in_specs=[smem, smem, smem, smem, vmem, vmem],
        out_specs=vmem,
        scratch_shapes=[pltpu.VMEM((row_width * col_width + 1, 64, 64), jnp.float32)],
        compiler_params=pltpu.CompilerParams(vmem_limit_bytes=24 * 2**20),
        name="local_terms",
    )(block_rows[0], block_cols[0], block_count, aggregate, prod, r_full)
    n_dev = n_row * n_col
    return pl.pallas_call(
        functools.partial(reduce_kernel, n_row, n_col, row_width),
        out_shape=jax.ShapeDtypeStruct((1, agg_total, 64, 64), jnp.float32),
        in_specs=[smem, vmem],
        out_specs=vmem,
        scratch_shapes=[
            pltpu.VMEM((2, row_width, 32, 128), jnp.float32),
            pltpu.VMEM((row_width, 32, 128), jnp.float32),
            pltpu.VMEM((n_col, 32, 128), jnp.bfloat16),
            pltpu.VMEM((n_dev, 32, 128), jnp.bfloat16),
            pltpu.SemaphoreType.DMA((2,)),
            pltpu.SemaphoreType.DMA((2,)),
            pltpu.SemaphoreType.DMA((n_dev,)),
            pltpu.SemaphoreType.DMA((n_dev,)),
        ],
        compiler_params=pltpu.CompilerParams(collective_id=1, has_side_effects=True, vmem_limit_bytes=limit),
        name="reduce_coarse",
    )(owner, part)


def solution(mesh):
    return jax.shard_map(
        functools.partial(on_device, mesh.shape["row"], mesh.shape["col"]),
        mesh=mesh,
        in_specs=(
            P("row", "col", None, None, None),
            P("row", "col", None),
            P("row", "col", None),
            P("row", "col"),
            P(("row", "col"), None, None),
            P("col", "row", None),
            P(),
            P(),
        ),
        out_specs=P("col", None, None, None),
        check_vma=False,
    )
```

```python
import functools

import jax
import jax.numpy as jnp
from jax import lax
from jax.experimental import pallas as pl
from jax.experimental.pallas import tpu as pltpu
from jax.sharding import PartitionSpec as P

MESH = pl.DeviceIdType.MESH
CORES = 2
DEPTH = 4


def gather_kernel(n_row, n_col, unroll, cols_ref, r_hbm, p_hbm, a_hbm, rg_ref, prod_ref, r_ref, p_ref, a_ref, pg_ref, flat, wide, load_sem, send_sem, recv_sem, psend_sem, precv_sem):
    width = n_col // (CORES * DEPTH)
    me = lax.axis_index("col")
    row = lax.axis_index("row")
    z = me // (width * CORES)
    x = lax.rem(me // CORES, width)
    k = lax.rem(me, CORES)
    sibling = me + 1 - 2 * k
    hop = width * CORES
    other_x = [(z * width + lax.rem(x + d, width)) * CORES + k for d in range(1, width)]
    other_row = [lax.rem(row + d, n_row) for d in range(1, n_row)]
    nb = r_ref.shape[0]
    half_p = p_ref.shape[0] // 2
    piece = p_ref.shape[1]
    slots = a_ref.shape[2]

    load_r = pltpu.make_async_copy(r_hbm, r_ref, load_sem.at[0])
    load_p = pltpu.make_async_copy(p_hbm, p_ref, load_sem.at[1])
    load_a = pltpu.make_async_copy(a_hbm, a_ref, load_sem.at[2])
    load_r.start()
    load_p.start()
    load_a.start()

    barrier = pltpu.get_barrier_semaphore()

    def greet(dev):
        pl.semaphore_signal(barrier, inc=1, device_id=dev, device_id_type=MESH)

    for o in other_row:
        greet((o, me))
    greet((row, sibling))
    for o in other_x:
        greet((row, o))

    @pl.when(z > 0)
    def _():
        greet((row, me - hop))

    @pl.when(z < DEPTH - 1)
    def _():
        greet((row, me + hop))

    load_r.wait()
    for i in range(nb):
        rg_ref[me, i, :, 0:64] = r_ref[i, 0:32]
        rg_ref[me, i, :, 64:128] = r_ref[i, 32:64]
    load_p.wait()
    for j in range(half_p):
        pg_ref[row, j, :, 0:64] = p_ref[j]
        pg_ref[row, j, :, 64:128] = p_ref[j + half_p]

    fixed = len(other_row) + 1 + len(other_x)
    pl.semaphore_wait(barrier, fixed + jnp.where(z > 0, 1, 0) + jnp.where(z < DEPTH - 1, 1, 0))

    def rcopy(shard, way, target):
        return pltpu.make_async_remote_copy(
            src_ref=rg_ref.at[shard],
            dst_ref=rg_ref.at[shard],
            send_sem=send_sem.at[shard, way],
            recv_sem=recv_sem.at[shard],
            device_id=(row, target),
            device_id_type=MESH,
        )

    def pcopy(way, target):
        return pltpu.make_async_remote_copy(
            src_ref=pg_ref.at[row],
            dst_ref=pg_ref.at[row],
            send_sem=psend_sem.at[way],
            recv_sem=precv_sem.at[row],
            device_id=(target, me),
            device_id_type=MESH,
        )

    def spread(shard):
        for w, o in enumerate(other_x):
            rcopy(shard, 3 + w, o).start()
        rcopy(shard, 0, sibling).start()

    @pl.when(z > 0)
    def _():
        rcopy(me, 1, me - hop).start()

    @pl.when(z < DEPTH - 1)
    def _():
        rcopy(me, 2, me + hop).start()

    for w, o in enumerate(other_row):
        pcopy(w, o).start()
    spread(me)

    def from_z(d):
        @pl.when(z - d >= 0)
        def _():
            shard = me - d * hop
            rcopy(shard, 0, sibling).wait_recv()

            @pl.when(z < DEPTH - 1)
            def _():
                rcopy(shard, 2, me + hop).start()

            spread(shard)

        @pl.when(z + d < DEPTH)
        def _():
            shard = me + d * hop
            rcopy(shard, 0, sibling).wait_recv()

            @pl.when(z > 0)
            def _():
                rcopy(shard, 1, me - hop).start()

            spread(shard)

    def from_x(d):
        for sign in ((1,) if d == 0 else (-1, 1)):
            @pl.when((z + sign * d >= 0) & (z + sign * d < DEPTH))
            def _():
                for o in other_x:
                    shard = o + sign * d * hop
                    rcopy(shard, 0, sibling).wait_recv()
                    rcopy(shard, 0, sibling).start()

    def turn(lo, hi):
        def body(i, _):
            for s in range(0, slots, 128):
                e = min(s + 128, slots)
                tall = jnp.concatenate([a_ref[i, :, s:e], a_ref[i + 32, :, s:e]], axis=0)
                flat[pl.ds(pl.multiple_of(i * slots + s, 8), e - s), :] = tall.astype(jnp.float32).T
            return 0

        lax.fori_loop(lo, hi, body, 0)

    def multiply(lo, hi):
        def body(g, _):
            base = g * unroll
            for u in range(unroll):
                p = base + u
                left = flat[pl.ds(p, 32, stride=slots), :].astype(jnp.bfloat16)
                prod_ref[p] = jnp.dot(
                    left, wide[cols_ref[0, p]], preferred_element_type=jnp.float32
                ).astype(jnp.bfloat16)
            return 0

        lax.fori_loop(lo, hi, body, 0)

    def widen(j, _):
        for r in range(n_row):
            lo, hi = r * piece, (r + 1) * piece
            both = pg_ref[r, j]
            wide[j, lo:hi, 0:64] = both[:, 0:64]
            wide[j, 64 + lo:64 + hi, 64:128] = both[:, 0:64]
            wide[j + half_p, lo:hi, 0:64] = both[:, 64:128]
            wide[j + half_p, 64 + lo:64 + hi, 64:128] = both[:, 64:128]
        return 0

    load_a.wait()
    turn(0, 12)
    from_z(1)
    turn(12, 22)
    from_x(0)
    turn(22, 32)
    from_z(2)
    for o in other_row:
        pltpu.make_async_remote_copy(
            src_ref=pg_ref.at[o], dst_ref=pg_ref.at[o], send_sem=psend_sem.at[0], recv_sem=precv_sem.at[o],
            device_id=(o, me), device_id_type=MESH,
        ).wait_recv()
    wide[...] = jnp.zeros_like(wide)
    lax.fori_loop(0, half_p, widen, 0, unroll=2)
    from_x(1)
    groups = slots // unroll
    multiply(0, groups // 4)
    from_z(3)
    multiply(groups // 4, groups // 2)
    from_x(2)
    multiply(groups // 2, 3 * groups // 4)
    from_x(3)
    multiply(3 * groups // 4, groups)

    for other in range(n_col // CORES):
        rcopy(other * CORES + 1 - k, 0, sibling).wait_recv()
    for other in range(n_col // CORES):
        rcopy(other * CORES + k, 0, sibling).wait_send()
    for zz in range(DEPTH):
        shard = (zz * width + x) * CORES + k
        for w in range(len(other_x)):
            rcopy(shard, 3 + w, me).wait_send()

        @pl.when((z > 0) & (zz >= z))
        def _():
            rcopy(shard, 1, me).wait_send()

        @pl.when((z < DEPTH - 1) & (zz <= z))
        def _():
            rcopy(shard, 2, me).wait_send()
    for w in range(len(other_row)):
        pcopy(w, row).wait_send()


def compute_kernel(n_row, n_col, row_width, col_width, unroll, rows_ref, cols_ref, count_ref, agg_ref, prod_ref, r_full, out_ref, acc):
    row = lax.axis_index("row")
    col = lax.axis_index("col")
    panel_rows = r_full.shape[0]
    panel_cols = agg_ref.shape[0] // n_col
    n_seg = row_width * col_width
    agg_total = n_col
    row_base = row * (agg_total // n_row) - 1
    col_base = col - 1

    acc[...] = jnp.zeros_like(acc)
    count = count_ref[0, 0]
    left_half = lax.broadcasted_iota(jnp.int32, (32, 128), 1) < 64
    none = jnp.zeros((32, 128), jnp.bfloat16)

    def group(g, _):
        base = g * unroll
        terms = []
        for u in range(unroll):
            both = prod_ref[base + u]
            turned = jnp.concatenate([both[:, 64:128], both[:, 0:64]], axis=1)
            right = jnp.concatenate(
                [
                    jnp.where(left_half, both, none),
                    jnp.where(left_half, turned, none),
                    jnp.where(left_half, none, turned),
                    jnp.where(left_half, none, both),
                ],
                axis=0,
            )
            terms.append(jnp.dot(r_full[rows_ref[0, base + u]], right, preferred_element_type=jnp.float32))
        for u in range(unroll):
            p = base + u
            ra = agg_ref[row * panel_rows + rows_ref[0, p]] - row_base
            ca = agg_ref[col * panel_cols + cols_ref[0, p]] - col_base
            seg = jnp.where(p < count, ra * col_width + ca, n_seg)
            acc[seg] += terms[u]
        return 0

    lax.fori_loop(0, pl.cdiv(count, unroll), group, 0)
    for ca in range(col_width):
        for ra in range(row_width):
            out_ref[ca, ra] = acc[ra * col_width + ca]


def reduce_kernel(n_row, n_col, row_width, owner_ref, part_ref, out_ref, edge, total, outgoing, incoming, inverse, esend_sem, erecv_sem, send_sem, recv_sem):
    row = lax.axis_index("row")
    col = lax.axis_index("col")
    n_dev = n_row * n_col
    me = row * n_col + col
    row_base = row * (n_col // n_row) - 1

    barrier = pltpu.get_barrier_semaphore()

    def greet(i, _):
        dev = lax.rem(me + i, n_dev)
        pl.semaphore_signal(barrier, inc=1, device_id=(dev // n_col, lax.rem(dev, n_col)), device_id_type=MESH)
        return 0

    lax.fori_loop(1, n_dev, greet, 0)
    pl.semaphore_wait(barrier, n_dev - 1)

    def ecopy(slot, side, target):
        return pltpu.make_async_remote_copy(
            src_ref=part_ref.at[slot], dst_ref=edge.at[side], send_sem=esend_sem.at[side], recv_sem=erecv_sem.at[side],
            device_id=(row, target), device_id_type=MESH,
        )

    down = ecopy(0, 1, col - 1)
    up = ecopy(2, 0, col + 1)

    @pl.when(col > 0)
    def _():
        down.start()

    @pl.when(col < n_col - 1)
    def _():
        up.start()

    total[...] = part_ref[1]

    def invert(s, _):
        inverse[s] = lax.fori_loop(0, n_col, lambda t, got: jnp.where(owner_ref[t] == s, t, got), 0, unroll=True)
        return 0

    lax.fori_loop(0, n_col, invert, 0)

    @pl.when(col > 0)
    def _():
        up.wait_recv()
        total[...] += edge[0]

    @pl.when(col < n_col - 1)
    def _():
        down.wait_recv()
        total[...] += edge[1]

    def dcopy(dev):
        return pltpu.make_async_remote_copy(
            src_ref=outgoing.at[lax.rem(dev, n_col)], dst_ref=incoming.at[me], send_sem=send_sem.at[dev], recv_sem=recv_sem.at[me],
            device_id=(dev // n_col, lax.rem(dev, n_col)), device_id_type=MESH,
        )

    def post(i, _):
        s = lax.rem(col + n_col // 2 + i, n_col)
        idx = inverse[s] - row_base
        valid = (idx >= 0) & (idx < row_width)
        block = total[jnp.clip(idx, 0, row_width - 1)]
        outgoing[s] = jnp.where(valid, block, 0.0).astype(jnp.bfloat16)
        for rr in range(n_row):
            dev = rr * n_col + s

            @pl.when(dev != me)
            def _():
                dcopy(dev).start()
        return 0

    lax.fori_loop(0, n_col, post, 0)
    incoming[me] = outgoing[col]

    def arrive(i, _):
        dev = lax.rem(me + i, n_dev)
        pltpu.make_async_remote_copy(
            src_ref=outgoing.at[0], dst_ref=incoming.at[dev], send_sem=send_sem.at[dev], recv_sem=recv_sem.at[dev],
            device_id=(dev // n_col, lax.rem(dev, n_col)), device_id_type=MESH,
        ).wait_recv()
        return 0

    lax.fori_loop(1, n_dev, arrive, 0)

    def emit(c, _):
        block = incoming[c].astype(jnp.float32)
        for rr in range(1, n_row):
            block += incoming[rr * n_col + c].astype(jnp.float32)
        out_ref[0, c, 0:32, :] = block[:, 0:64]
        out_ref[0, c, 32:64, :] = block[:, 64:128]
        return 0

    lax.fori_loop(0, n_col, emit, 0)

    def sent(i, _):
        dcopy(lax.rem(me + i, n_dev)).wait_send()
        return 0

    lax.fori_loop(1, n_dev, sent, 0)

    @pl.when(col > 0)
    def _():
        down.wait_send()

    @pl.when(col < n_col - 1)
    def _():
        up.wait_send()


def on_device(n_row, n_col, a_blocks, block_rows, block_cols, block_count, restrict, interp, aggregate, owner):
    vmem = pl.BlockSpec(memory_space=pltpu.VMEM)
    smem = pl.BlockSpec(memory_space=pltpu.SMEM)
    width = n_col // (CORES * DEPTH)
    nb = restrict.shape[0]
    nj, piece = interp.shape[:2]
    slots = a_blocks.shape[2]
    agg_total = owner.shape[0]
    assert agg_total == n_col
    row_width = agg_total // n_row + 2
    col_width = 3
    limit = 40 * 2**20
    hbm = pl.BlockSpec(memory_space=pltpu.HBM)
    sized = jnp.transpose(a_blocks[0, 0], (1, 2, 0))
    rg, prod = pl.pallas_call(
        functools.partial(gather_kernel, n_row, n_col, 8),
        out_shape=(
            jax.ShapeDtypeStruct((n_col, nb, 32, 128), jnp.bfloat16),
            jax.ShapeDtypeStruct((slots, 32, 128), jnp.bfloat16),
        ),
        in_specs=[smem, hbm, hbm, hbm],
        out_specs=(vmem, vmem),
        scratch_shapes=[
            pltpu.VMEM((nb, 64, 64), jnp.bfloat16),
            pltpu.VMEM((nj, piece, 64), jnp.bfloat16),
            pltpu.VMEM((64, 64, slots), jnp.bfloat16),
            pltpu.VMEM((n_row, nj // 2, piece, 128), jnp.bfloat16),
            pltpu.VMEM((32 * slots, 128), jnp.float32),
            pltpu.VMEM((nj, 128, 128), jnp.bfloat16),
            pltpu.SemaphoreType.DMA((3,)),
            pltpu.SemaphoreType.DMA((n_col, 3 + width)),
            pltpu.SemaphoreType.DMA((n_col,)),
            pltpu.SemaphoreType.DMA((n_row,)),
            pltpu.SemaphoreType.DMA((n_row,)),
        ],
        compiler_params=pltpu.CompilerParams(collective_id=0, has_side_effects=True, vmem_limit_bytes=50_000_000),
        name="gather_panels",
    )(block_cols[0], restrict, interp, sized)
    part = pl.pallas_call(
        functools.partial(compute_kernel, n_row, n_col, row_width, col_width, 16),
        out_shape=jax.ShapeDtypeStruct((col_width, row_width, 32, 128), jnp.float32),
        in_specs=[smem, smem, smem, smem, vmem, vmem],
        out_specs=vmem,
        scratch_shapes=[pltpu.VMEM((row_width * col_width + 1, 32, 128), jnp.float32)],
        compiler_params=pltpu.CompilerParams(vmem_limit_bytes=24 * 2**20),
        name="local_terms",
    )(block_rows[0], block_cols[0], block_count, aggregate, prod, rg.reshape(n_col * nb, 32, 128))
    n_dev = n_row * n_col
    return pl.pallas_call(
        functools.partial(reduce_kernel, n_row, n_col, row_width),
        out_shape=jax.ShapeDtypeStruct((1, agg_total, 64, 64), jnp.float32),
        in_specs=[smem, vmem],
        out_specs=vmem,
        scratch_shapes=[
            pltpu.VMEM((2, row_width, 32, 128), jnp.float32),
            pltpu.VMEM((row_width, 32, 128), jnp.float32),
            pltpu.VMEM((n_col, 32, 128), jnp.bfloat16),
            pltpu.VMEM((n_dev, 32, 128), jnp.bfloat16),
            pltpu.SMEM((n_col,), jnp.int32),
            pltpu.SemaphoreType.DMA((2,)),
            pltpu.SemaphoreType.DMA((2,)),
            pltpu.SemaphoreType.DMA((n_dev,)),
            pltpu.SemaphoreType.DMA((n_dev,)),
        ],
        compiler_params=pltpu.CompilerParams(collective_id=1, has_side_effects=True, vmem_limit_bytes=limit),
        name="reduce_coarse",
    )(owner, part)


def solution(mesh):
    return jax.shard_map(
        functools.partial(on_device, mesh.shape["row"], mesh.shape["col"]),
        mesh=mesh,
        in_specs=(
            P("row", "col", None, None, None),
            P("row", "col", None),
            P("row", "col", None),
            P("row", "col"),
            P(("row", "col"), None, None),
            P("col", "row", None),
            P(),
            P(),
        ),
        out_specs=P("col", None, None, None),
        check_vma=False,
    )
```

```python
import functools

import jax
import jax.numpy as jnp
from jax import lax
from jax.experimental import pallas as pl
from jax.experimental.pallas import tpu as pltpu
from jax.sharding import PartitionSpec as P

MESH = pl.DeviceIdType.MESH
CORES = 2
DEPTH = 4


def gather_kernel(n_row, n_col, unroll, cols_ref, r_hbm, p_hbm, a_hbm, rg_ref, prod_ref, r_ref, p_ref, a_ref, pg_ref, flat, wide, load_sem, send_sem, recv_sem, psend_sem, precv_sem):
    width = n_col // (CORES * DEPTH)
    me = lax.axis_index("col")
    row = lax.axis_index("row")
    z = me // (width * CORES)
    x = lax.rem(me // CORES, width)
    k = lax.rem(me, CORES)
    sibling = me + 1 - 2 * k
    hop = width * CORES
    other_x = [(z * width + lax.rem(x + d, width)) * CORES + k for d in range(1, width)]
    other_row = [lax.rem(row + d, n_row) for d in range(1, n_row)]
    nb = r_ref.shape[0]
    half_p = p_ref.shape[0] // 2
    piece = p_ref.shape[1]
    slots = a_ref.shape[2]

    load_r = pltpu.make_async_copy(r_hbm, r_ref, load_sem.at[0])
    load_p = pltpu.make_async_copy(p_hbm, p_ref, load_sem.at[1])
    load_a = pltpu.make_async_copy(a_hbm, a_ref, load_sem.at[2])
    load_r.start()
    load_p.start()
    load_a.start()

    barrier = pltpu.get_barrier_semaphore()

    def greet(dev):
        pl.semaphore_signal(barrier, inc=1, device_id=dev, device_id_type=MESH)

    for o in other_row:
        greet((o, me))
    greet((row, sibling))
    for o in other_x:
        greet((row, o))

    @pl.when(z > 0)
    def _():
        greet((row, me - hop))

    @pl.when(z < DEPTH - 1)
    def _():
        greet((row, me + hop))

    load_r.wait()
    for i in range(nb):
        rg_ref[me, i, :, 0:64] = r_ref[i, 0:32]
        rg_ref[me, i, :, 64:128] = r_ref[i, 32:64]
    load_p.wait()
    for j in range(half_p):
        pg_ref[row, j, :, 0:64] = p_ref[j]
        pg_ref[row, j, :, 64:128] = p_ref[j + half_p]

    fixed = len(other_row) + 1 + len(other_x)
    pl.semaphore_wait(barrier, fixed + jnp.where(z > 0, 1, 0) + jnp.where(z < DEPTH - 1, 1, 0))

    def rcopy(shard, way, target):
        return pltpu.make_async_remote_copy(
            src_ref=rg_ref.at[shard],
            dst_ref=rg_ref.at[shard],
            send_sem=send_sem.at[shard, way],
            recv_sem=recv_sem.at[shard],
            device_id=(row, target),
            device_id_type=MESH,
        )

    def pcopy(way, target):
        return pltpu.make_async_remote_copy(
            src_ref=pg_ref.at[row],
            dst_ref=pg_ref.at[row],
            send_sem=psend_sem.at[way],
            recv_sem=precv_sem.at[row],
            device_id=(target, me),
            device_id_type=MESH,
        )

    def spread(shard):
        for w, o in enumerate(other_x):
            rcopy(shard, 3 + w, o).start()
        rcopy(shard, 0, sibling).start()

    @pl.when(z > 0)
    def _():
        rcopy(me, 1, me - hop).start()

    @pl.when(z < DEPTH - 1)
    def _():
        rcopy(me, 2, me + hop).start()

    for w, o in enumerate(other_row):
        pcopy(w, o).start()
    spread(me)

    def from_z(d):
        @pl.when(z - d >= 0)
        def _():
            shard = me - d * hop
            rcopy(shard, 0, sibling).wait_recv()

            @pl.when(z < DEPTH - 1)
            def _():
                rcopy(shard, 2, me + hop).start()

            spread(shard)

        @pl.when(z + d < DEPTH)
        def _():
            shard = me + d * hop
            rcopy(shard, 0, sibling).wait_recv()

            @pl.when(z > 0)
            def _():
                rcopy(shard, 1, me - hop).start()

            spread(shard)

    def from_x(d):
        for sign in ((1,) if d == 0 else (-1, 1)):
            @pl.when((z + sign * d >= 0) & (z + sign * d < DEPTH))
            def _():
                for o in other_x:
                    shard = o + sign * d * hop
                    rcopy(shard, 0, sibling).wait_recv()
                    rcopy(shard, 0, sibling).start()

    def turn(lo, hi):
        def body(i, _):
            for s in range(0, slots, 128):
                e = min(s + 128, slots)
                tall = jnp.concatenate([a_ref[i, :, s:e], a_ref[i + 32, :, s:e]], axis=0)
                flat[pl.ds(pl.multiple_of(i * slots + s, 8), e - s), :] = tall.astype(jnp.float32).T
            return 0

        lax.fori_loop(lo, hi, body, 0)

    def multiply(lo, hi):
        def body(g, _):
            base = g * unroll
            for u in range(unroll):
                p = base + u
                left = flat[pl.ds(p, 32, stride=slots), :].astype(jnp.bfloat16)
                prod_ref[p] = jnp.dot(
                    left, wide[cols_ref[0, p]], preferred_element_type=jnp.float32
                ).astype(jnp.bfloat16)
            return 0

        lax.fori_loop(lo, hi, body, 0)

    def widen(j, _):
        for r in range(n_row):
            lo, hi = r * piece, (r + 1) * piece
            both = pg_ref[r, j]
            wide[j, lo:hi, 0:64] = both[:, 0:64]
            wide[j, 64 + lo:64 + hi, 64:128] = both[:, 0:64]
            wide[j + half_p, lo:hi, 0:64] = both[:, 64:128]
            wide[j + half_p, 64 + lo:64 + hi, 64:128] = both[:, 64:128]
        return 0

    load_a.wait()
    turn(0, 12)
    from_z(1)
    turn(12, 22)
    from_x(0)
    turn(22, 32)
    from_z(2)
    for o in other_row:
        pltpu.make_async_remote_copy(
            src_ref=pg_ref.at[o], dst_ref=pg_ref.at[o], send_sem=psend_sem.at[0], recv_sem=precv_sem.at[o],
            device_id=(o, me), device_id_type=MESH,
        ).wait_recv()
    wide[...] = jnp.zeros_like(wide)
    lax.fori_loop(0, half_p, widen, 0, unroll=2)
    from_x(1)
    groups = slots // unroll
    multiply(0, groups // 4)
    from_z(3)
    multiply(groups // 4, groups // 2)
    from_x(2)
    multiply(groups // 2, 3 * groups // 4)
    from_x(3)
    multiply(3 * groups // 4, groups)

    for other in range(n_col // CORES):
        rcopy(other * CORES + 1 - k, 0, sibling).wait_recv()
    for other in range(n_col // CORES):
        rcopy(other * CORES + k, 0, sibling).wait_send()
    for zz in range(DEPTH):
        shard = (zz * width + x) * CORES + k
        for w in range(len(other_x)):
            rcopy(shard, 3 + w, me).wait_send()

        @pl.when((z > 0) & (zz >= z))
        def _():
            rcopy(shard, 1, me).wait_send()

        @pl.when((z < DEPTH - 1) & (zz <= z))
        def _():
            rcopy(shard, 2, me).wait_send()
    for w in range(len(other_row)):
        pcopy(w, row).wait_send()


def compute_kernel(n_row, n_col, row_width, col_width, unroll, rows_ref, cols_ref, count_ref, agg_ref, prod_ref, r_full, out_ref, acc):
    row = lax.axis_index("row")
    col = lax.axis_index("col")
    panel_rows = r_full.shape[0]
    panel_cols = agg_ref.shape[0] // n_col
    n_seg = row_width * col_width
    agg_total = n_col
    row_base = row * (agg_total // n_row) - 1
    col_base = col - 1

    acc[...] = jnp.zeros_like(acc)
    count = count_ref[0, 0]
    left_half = lax.broadcasted_iota(jnp.int32, (32, 128), 1) < 64
    none = jnp.zeros((32, 128), jnp.bfloat16)

    def group(g, _):
        base = g * unroll
        terms = []
        for u in range(unroll):
            both = prod_ref[base + u]
            turned = jnp.concatenate([both[:, 64:128], both[:, 0:64]], axis=1)
            right = jnp.concatenate(
                [
                    jnp.where(left_half, both, none),
                    jnp.where(left_half, turned, none),
                    jnp.where(left_half, none, turned),
                    jnp.where(left_half, none, both),
                ],
                axis=0,
            )
            terms.append(jnp.dot(r_full[rows_ref[0, base + u]], right, preferred_element_type=jnp.float32))
        for u in range(unroll):
            p = base + u
            ra = agg_ref[row * panel_rows + rows_ref[0, p]] - row_base
            ca = agg_ref[col * panel_cols + cols_ref[0, p]] - col_base
            seg = jnp.where(p < count, ra * col_width + ca, n_seg)
            acc[seg] += terms[u]
        return 0

    lax.fori_loop(0, pl.cdiv(count, unroll), group, 0)
    for ca in range(col_width):
        for ra in range(row_width):
            out_ref[ca, ra] = acc[ra * col_width + ca]


def reduce_kernel(n_row, n_col, row_width, owner_ref, part_ref, out_ref, away, edge, rows_in, outgoing, incoming, full, inverse, esend_sem, erecv_sem, rsend_sem, rrecv_sem, send_sem, recv_sem):
    row = lax.axis_index("row")
    col = lax.axis_index("col")
    panel_agg = n_col // n_row
    others = [lax.rem(row + d, n_row) for d in range(1, n_row)]

    barrier = pltpu.get_barrier_semaphore()

    def greet(i, _):
        pl.semaphore_signal(barrier, inc=1, device_id=(row, lax.rem(col + i, n_col)), device_id_type=MESH)
        return 0

    lax.fori_loop(1, n_col, greet, 0)
    for o in others:
        pl.semaphore_signal(barrier, inc=1, device_id=(o, col), device_id_type=MESH)
    away[0] = part_ref[0].astype(jnp.bfloat16)
    away[1] = part_ref[2].astype(jnp.bfloat16)
    pl.semaphore_wait(barrier, n_col - 1 + len(others))

    def ecopy(side, target):
        return pltpu.make_async_remote_copy(
            src_ref=away.at[side], dst_ref=edge.at[side], send_sem=esend_sem.at[side], recv_sem=erecv_sem.at[side],
            device_id=(row, target), device_id_type=MESH,
        )

    down = ecopy(0, col - 1)
    up = ecopy(1, col + 1)

    @pl.when(col > 0)
    def _():
        down.start()

    @pl.when(col < n_col - 1)
    def _():
        up.start()

    def invert(s, _):
        inverse[s] = lax.fori_loop(0, n_col, lambda t, got: jnp.where(owner_ref[t] == s, t, got), 0, unroll=True)
        return 0

    lax.fori_loop(0, n_col, invert, 0)

    @pl.when(col == 0)
    def _():
        edge[1] = jnp.zeros_like(edge[1])

    @pl.when(col == n_col - 1)
    def _():
        edge[0] = jnp.zeros_like(edge[0])

    @pl.when(col > 0)
    def _():
        up.wait_recv()

    @pl.when(col < n_col - 1)
    def _():
        down.wait_recv()

    rows_in[row] = (part_ref[1] + edge[0].astype(jnp.float32) + edge[1].astype(jnp.float32)).astype(jnp.bfloat16)

    def rcopy(way, source, target):
        return pltpu.make_async_remote_copy(
            src_ref=rows_in.at[source], dst_ref=rows_in.at[source], send_sem=rsend_sem.at[way], recv_sem=rrecv_sem.at[source],
            device_id=(target, col), device_id_type=MESH,
        )

    for w, o in enumerate(others):
        rcopy(w, row, o).start()
    for o in others:
        rcopy(0, o, o).wait_recv()
    for a in range(n_col):
        pieces = [
            rows_in[r, a - r * panel_agg + 1].astype(jnp.float32)
            for r in range(n_row)
            if 0 <= a - r * panel_agg + 1 < row_width
        ]
        full[a] = functools.reduce(jnp.add, pieces).astype(jnp.bfloat16)

    def dcopy(s):
        return pltpu.make_async_remote_copy(
            src_ref=outgoing.at[s], dst_ref=incoming.at[col], send_sem=send_sem.at[s], recv_sem=recv_sem.at[col],
            device_id=(row, s), device_id_type=MESH,
        )

    def post(i, _):
        s = lax.rem(col + i, n_col)
        outgoing[s] = full[inverse[s]]
        dcopy(s).start()
        return 0

    lax.fori_loop(1, n_col, post, 0)
    incoming[col] = full[inverse[col]]

    def emit(c):
        block = incoming[c].astype(jnp.float32)
        out_ref[0, c, 0:32, :] = block[:, 0:64]
        out_ref[0, c, 32:64, :] = block[:, 64:128]

    emit(col)

    def arrive(i, _):
        c = lax.rem(col + n_col - i, n_col)
        pltpu.make_async_remote_copy(
            src_ref=outgoing.at[0], dst_ref=incoming.at[c], send_sem=send_sem.at[c], recv_sem=recv_sem.at[c],
            device_id=(row, c), device_id_type=MESH,
        ).wait_recv()
        emit(c)
        return 0

    lax.fori_loop(1, n_col, arrive, 0)

    def sent(i, _):
        dcopy(lax.rem(col + i, n_col)).wait_send()
        return 0

    lax.fori_loop(1, n_col, sent, 0)
    for w, o in enumerate(others):
        rcopy(w, row, o).wait_send()

    @pl.when(col > 0)
    def _():
        down.wait_send()

    @pl.when(col < n_col - 1)
    def _():
        up.wait_send()


def on_device(n_row, n_col, a_blocks, block_rows, block_cols, block_count, restrict, interp, aggregate, owner):
    vmem = pl.BlockSpec(memory_space=pltpu.VMEM)
    smem = pl.BlockSpec(memory_space=pltpu.SMEM)
    width = n_col // (CORES * DEPTH)
    nb = restrict.shape[0]
    nj, piece = interp.shape[:2]
    slots = a_blocks.shape[2]
    agg_total = owner.shape[0]
    assert agg_total == n_col
    row_width = agg_total // n_row + 2
    col_width = 3
    limit = 40 * 2**20
    hbm = pl.BlockSpec(memory_space=pltpu.HBM)
    sized = jnp.transpose(a_blocks[0, 0], (1, 2, 0))
    rg, prod = pl.pallas_call(
        functools.partial(gather_kernel, n_row, n_col, 8),
        out_shape=(
            jax.ShapeDtypeStruct((n_col, nb, 32, 128), jnp.bfloat16),
            jax.ShapeDtypeStruct((slots, 32, 128), jnp.bfloat16),
        ),
        in_specs=[smem, hbm, hbm, hbm],
        out_specs=(vmem, vmem),
        scratch_shapes=[
            pltpu.VMEM((nb, 64, 64), jnp.bfloat16),
            pltpu.VMEM((nj, piece, 64), jnp.bfloat16),
            pltpu.VMEM((64, 64, slots), jnp.bfloat16),
            pltpu.VMEM((n_row, nj // 2, piece, 128), jnp.bfloat16),
            pltpu.VMEM((32 * slots, 128), jnp.float32),
            pltpu.VMEM((nj, 128, 128), jnp.bfloat16),
            pltpu.SemaphoreType.DMA((3,)),
            pltpu.SemaphoreType.DMA((n_col, 3 + width)),
            pltpu.SemaphoreType.DMA((n_col,)),
            pltpu.SemaphoreType.DMA((n_row,)),
            pltpu.SemaphoreType.DMA((n_row,)),
        ],
        compiler_params=pltpu.CompilerParams(collective_id=0, has_side_effects=True, vmem_limit_bytes=50_000_000),
        name="gather_panels",
    )(block_cols[0], restrict, interp, sized)
    part = pl.pallas_call(
        functools.partial(compute_kernel, n_row, n_col, row_width, col_width, 16),
        out_shape=jax.ShapeDtypeStruct((col_width, row_width, 32, 128), jnp.float32),
        in_specs=[smem, smem, smem, smem, vmem, vmem],
        out_specs=vmem,
        scratch_shapes=[pltpu.VMEM((row_width * col_width + 1, 32, 128), jnp.float32)],
        compiler_params=pltpu.CompilerParams(vmem_limit_bytes=24 * 2**20),
        name="local_terms",
    )(block_rows[0], block_cols[0], block_count, aggregate, prod, rg.reshape(n_col * nb, 32, 128))
    return pl.pallas_call(
        functools.partial(reduce_kernel, n_row, n_col, row_width),
        out_shape=jax.ShapeDtypeStruct((1, agg_total, 64, 64), jnp.float32),
        in_specs=[smem, vmem],
        out_specs=vmem,
        scratch_shapes=[
            pltpu.VMEM((2, row_width, 32, 128), jnp.bfloat16),
            pltpu.VMEM((2, row_width, 32, 128), jnp.bfloat16),
            pltpu.VMEM((n_row, row_width, 32, 128), jnp.bfloat16),
            pltpu.VMEM((n_col, 32, 128), jnp.bfloat16),
            pltpu.VMEM((n_col, 32, 128), jnp.bfloat16),
            pltpu.VMEM((n_col, 32, 128), jnp.bfloat16),
            pltpu.SMEM((n_col,), jnp.int32),
            pltpu.SemaphoreType.DMA((2,)),
            pltpu.SemaphoreType.DMA((2,)),
            pltpu.SemaphoreType.DMA((n_row,)),
            pltpu.SemaphoreType.DMA((n_row,)),
            pltpu.SemaphoreType.DMA((n_col,)),
            pltpu.SemaphoreType.DMA((n_col,)),
        ],
        compiler_params=pltpu.CompilerParams(collective_id=1, has_side_effects=True, vmem_limit_bytes=limit),
        name="reduce_coarse",
    )(owner, part)


def solution(mesh):
    return jax.shard_map(
        functools.partial(on_device, mesh.shape["row"], mesh.shape["col"]),
        mesh=mesh,
        in_specs=(
            P("row", "col", None, None, None),
            P("row", "col", None),
            P("row", "col", None),
            P("row", "col"),
            P(("row", "col"), None, None),
            P("col", "row", None),
            P(),
            P(),
        ),
        out_specs=P("col", None, None, None),
        check_vma=False,
    )
```

```python
import functools

import jax
import jax.numpy as jnp
from jax import lax
from jax.experimental import pallas as pl
from jax.experimental.pallas import tpu as pltpu
from jax.sharding import PartitionSpec as P

MESH = pl.DeviceIdType.MESH
CORES = 2
DEPTH = 4


def gather_kernel(n_row, n_col, unroll, cols_ref, r_hbm, p_hbm, a_hbm, rg_ref, prod_ref, r_ref, p_ref, a_ref, pg_ref, flat, wide, load_sem, send_sem, recv_sem, psend_sem, precv_sem):
    width = n_col // (CORES * DEPTH)
    me = lax.axis_index("col")
    row = lax.axis_index("row")
    z = me // (width * CORES)
    x = lax.rem(me // CORES, width)
    k = lax.rem(me, CORES)
    sibling = me + 1 - 2 * k
    hop = width * CORES
    other_x = [(z * width + lax.rem(x + d, width)) * CORES + k for d in range(1, width)]
    other_row = [lax.rem(row + d, n_row) for d in range(1, n_row)]
    nb = r_ref.shape[0]
    half_p = p_ref.shape[0] // 2
    piece = p_ref.shape[1]
    slots = a_ref.shape[2]

    load_r = pltpu.make_async_copy(r_hbm, r_ref, load_sem.at[0])
    load_p = pltpu.make_async_copy(p_hbm, p_ref, load_sem.at[1])
    load_a = pltpu.make_async_copy(a_hbm, a_ref, load_sem.at[2])
    load_r.start()
    load_p.start()
    load_a.start()

    barrier = pltpu.get_barrier_semaphore()

    def greet(dev):
        pl.semaphore_signal(barrier, inc=1, device_id=dev, device_id_type=MESH)

    for o in other_row:
        greet((o, me))
    greet((row, sibling))
    for o in other_x:
        greet((row, o))

    @pl.when(z > 0)
    def _():
        greet((row, me - hop))

    @pl.when(z < DEPTH - 1)
    def _():
        greet((row, me + hop))

    load_r.wait()
    for i in range(nb):
        rg_ref[me, i, :, 0:64] = r_ref[i, 0:32]
        rg_ref[me, i, :, 64:128] = r_ref[i, 32:64]
    load_p.wait()
    for j in range(half_p):
        pg_ref[row, j, :, 0:64] = p_ref[j]
        pg_ref[row, j, :, 64:128] = p_ref[j + half_p]

    fixed = len(other_row) + 1 + len(other_x)
    pl.semaphore_wait(barrier, fixed + jnp.where(z > 0, 1, 0) + jnp.where(z < DEPTH - 1, 1, 0))

    def rcopy(shard, way, target):
        return pltpu.make_async_remote_copy(
            src_ref=rg_ref.at[shard],
            dst_ref=rg_ref.at[shard],
            send_sem=send_sem.at[shard, way],
            recv_sem=recv_sem.at[shard],
            device_id=(row, target),
            device_id_type=MESH,
        )

    def pcopy(way, target):
        return pltpu.make_async_remote_copy(
            src_ref=pg_ref.at[row],
            dst_ref=pg_ref.at[row],
            send_sem=psend_sem.at[way],
            recv_sem=precv_sem.at[row],
            device_id=(target, me),
            device_id_type=MESH,
        )

    def spread(shard):
        for w, o in enumerate(other_x):
            rcopy(shard, 3 + w, o).start()
        rcopy(shard, 0, sibling).start()

    @pl.when(z > 0)
    def _():
        rcopy(me, 1, me - hop).start()

    @pl.when(z < DEPTH - 1)
    def _():
        rcopy(me, 2, me + hop).start()

    for w, o in enumerate(other_row):
        pcopy(w, o).start()
    spread(me)

    def from_z(d):
        @pl.when(z - d >= 0)
        def _():
            shard = me - d * hop
            rcopy(shard, 0, sibling).wait_recv()

            @pl.when(z < DEPTH - 1)
            def _():
                rcopy(shard, 2, me + hop).start()

            spread(shard)

        @pl.when(z + d < DEPTH)
        def _():
            shard = me + d * hop
            rcopy(shard, 0, sibling).wait_recv()

            @pl.when(z > 0)
            def _():
                rcopy(shard, 1, me - hop).start()

            spread(shard)

    def from_x(d):
        for sign in ((1,) if d == 0 else (-1, 1)):
            @pl.when((z + sign * d >= 0) & (z + sign * d < DEPTH))
            def _():
                for o in other_x:
                    shard = o + sign * d * hop
                    rcopy(shard, 0, sibling).wait_recv()
                    rcopy(shard, 0, sibling).start()

    def turn(lo, hi):
        def body(i, _):
            for s in range(0, slots, 128):
                e = min(s + 128, slots)
                tall = jnp.concatenate([a_ref[i, :, s:e], a_ref[i + 32, :, s:e]], axis=0)
                flat[pl.ds(pl.multiple_of(i * slots + s, 8), e - s), :] = tall.astype(jnp.float32).T
            return 0

        lax.fori_loop(lo, hi, body, 0)

    def multiply(lo, hi):
        def body(g, _):
            base = g * unroll
            for u in range(unroll):
                p = base + u
                left = flat[pl.ds(p, 32, stride=slots), :].astype(jnp.bfloat16)
                prod_ref[p] = jnp.dot(
                    left, wide[cols_ref[0, p]], preferred_element_type=jnp.float32
                ).astype(jnp.bfloat16)
            return 0

        lax.fori_loop(lo, hi, body, 0)

    def widen(j, _):
        for r in range(n_row):
            lo, hi = r * piece, (r + 1) * piece
            both = pg_ref[r, j]
            wide[j, lo:hi, 0:64] = both[:, 0:64]
            wide[j, 64 + lo:64 + hi, 64:128] = both[:, 0:64]
            wide[j + half_p, lo:hi, 0:64] = both[:, 64:128]
            wide[j + half_p, 64 + lo:64 + hi, 64:128] = both[:, 64:128]
        return 0

    load_a.wait()
    turn(0, 12)
    from_z(1)
    turn(12, 22)
    from_x(0)
    turn(22, 32)
    from_z(2)
    for o in other_row:
        pltpu.make_async_remote_copy(
            src_ref=pg_ref.at[o], dst_ref=pg_ref.at[o], send_sem=psend_sem.at[0], recv_sem=precv_sem.at[o],
            device_id=(o, me), device_id_type=MESH,
        ).wait_recv()
    wide[...] = jnp.zeros_like(wide)
    lax.fori_loop(0, half_p, widen, 0, unroll=2)
    from_x(1)
    groups = slots // unroll
    multiply(0, groups // 4)
    from_z(3)
    multiply(groups // 4, groups // 2)
    from_x(2)
    multiply(groups // 2, 3 * groups // 4)
    from_x(3)
    multiply(3 * groups // 4, groups)

    for other in range(n_col // CORES):
        rcopy(other * CORES + 1 - k, 0, sibling).wait_recv()
    for other in range(n_col // CORES):
        rcopy(other * CORES + k, 0, sibling).wait_send()
    for zz in range(DEPTH):
        shard = (zz * width + x) * CORES + k
        for w in range(len(other_x)):
            rcopy(shard, 3 + w, me).wait_send()

        @pl.when((z > 0) & (zz >= z))
        def _():
            rcopy(shard, 1, me).wait_send()

        @pl.when((z < DEPTH - 1) & (zz <= z))
        def _():
            rcopy(shard, 2, me).wait_send()
    for w in range(len(other_row)):
        pcopy(w, row).wait_send()


def compute_kernel(n_row, n_col, row_width, col_width, unroll, rows_ref, cols_ref, count_ref, agg_ref, prod_ref, r_full, out_ref, acc):
    row = lax.axis_index("row")
    col = lax.axis_index("col")
    panel_rows = r_full.shape[0]
    panel_cols = agg_ref.shape[0] // n_col
    n_seg = row_width * col_width
    agg_total = n_col
    row_base = row * (agg_total // n_row) - 1
    col_base = col - 1

    acc[...] = jnp.zeros_like(acc)
    count = count_ref[0, 0]
    left_half = lax.broadcasted_iota(jnp.int32, (32, 128), 1) < 64
    none = jnp.zeros((32, 128), jnp.bfloat16)

    def group(g, _):
        base = g * unroll
        terms = []
        for u in range(unroll):
            both = prod_ref[base + u]
            turned = jnp.concatenate([both[:, 64:128], both[:, 0:64]], axis=1)
            right = jnp.concatenate(
                [
                    jnp.where(left_half, both, none),
                    jnp.where(left_half, turned, none),
                    jnp.where(left_half, none, turned),
                    jnp.where(left_half, none, both),
                ],
                axis=0,
            )
            terms.append(jnp.dot(r_full[rows_ref[0, base + u]], right, preferred_element_type=jnp.float32))
        for u in range(unroll):
            p = base + u
            ra = agg_ref[row * panel_rows + rows_ref[0, p]] - row_base
            ca = agg_ref[col * panel_cols + cols_ref[0, p]] - col_base
            seg = jnp.where(p < count, ra * col_width + ca, n_seg)
            acc[seg] += terms[u]
        return 0

    lax.fori_loop(0, pl.cdiv(count, unroll), group, 0)
    for ca in range(col_width):
        for ra in range(row_width):
            out_ref[ca, ra] = acc[ra * col_width + ca]


def reduce_kernel(n_row, n_col, row_width, owner_ref, part_ref, out_ref, away, edge, rows_in, outgoing, incoming, full, inverse, esend_sem, erecv_sem, rsend_sem, rrecv_sem, send_sem, recv_sem):
    row = lax.axis_index("row")
    col = lax.axis_index("col")
    panel_agg = n_col // n_row
    others = [lax.rem(row + d, n_row) for d in range(1, n_row)]

    barrier = pltpu.get_barrier_semaphore()

    def greet(i, _):
        pl.semaphore_signal(barrier, inc=1, device_id=(row, lax.rem(col + i, n_col)), device_id_type=MESH)
        return 0

    lax.fori_loop(1, n_col, greet, 0)
    for o in others:
        pl.semaphore_signal(barrier, inc=1, device_id=(o, col), device_id_type=MESH)
    away[0] = part_ref[0].astype(jnp.bfloat16)
    away[1] = part_ref[2].astype(jnp.bfloat16)
    pl.semaphore_wait(barrier, n_col - 1 + len(others))

    def ecopy(side, target):
        return pltpu.make_async_remote_copy(
            src_ref=away.at[side], dst_ref=edge.at[side], send_sem=esend_sem.at[side], recv_sem=erecv_sem.at[side],
            device_id=(row, target), device_id_type=MESH,
        )

    down = ecopy(0, col - 1)
    up = ecopy(1, col + 1)

    @pl.when(col > 0)
    def _():
        down.start()

    @pl.when(col < n_col - 1)
    def _():
        up.start()

    def invert(s, _):
        inverse[s] = lax.fori_loop(0, n_col, lambda t, got: jnp.where(owner_ref[t] == s, t, got), 0, unroll=True)
        return 0

    lax.fori_loop(0, n_col, invert, 0)

    @pl.when(col == 0)
    def _():
        edge[1] = jnp.zeros_like(edge[1])

    @pl.when(col == n_col - 1)
    def _():
        edge[0] = jnp.zeros_like(edge[0])

    @pl.when(col > 0)
    def _():
        up.wait_recv()

    @pl.when(col < n_col - 1)
    def _():
        down.wait_recv()

    rows_in[row] = (part_ref[1] + edge[0].astype(jnp.float32) + edge[1].astype(jnp.float32)).astype(jnp.bfloat16)

    def rcopy(way, source, target):
        return pltpu.make_async_remote_copy(
            src_ref=rows_in.at[source], dst_ref=rows_in.at[source], send_sem=rsend_sem.at[way], recv_sem=rrecv_sem.at[source],
            device_id=(target, col), device_id_type=MESH,
        )

    for w, o in enumerate(others):
        rcopy(w, row, o).start()
    for o in others:
        rcopy(0, o, o).wait_recv()
    for a in range(n_col):
        pieces = [
            rows_in[r, a - r * panel_agg + 1].astype(jnp.float32)
            for r in range(n_row)
            if 0 <= a - r * panel_agg + 1 < row_width
        ]
        full[a] = functools.reduce(jnp.add, pieces).astype(jnp.bfloat16)

    def dcopy(s):
        return pltpu.make_async_remote_copy(
            src_ref=outgoing.at[s], dst_ref=incoming.at[col], send_sem=send_sem.at[s], recv_sem=recv_sem.at[col],
            device_id=(row, s), device_id_type=MESH,
        )

    def post(i, _):
        s = lax.rem(col + i, n_col)
        outgoing[s] = full[inverse[s]]
        dcopy(s).start()
        return 0

    lax.fori_loop(1, n_col, post, 0)
    incoming[col] = full[inverse[col]]

    def emit(c):
        block = incoming[c].astype(jnp.float32)
        out_ref[0, c, 0:32, :] = block[:, 0:64]
        out_ref[0, c, 32:64, :] = block[:, 64:128]

    emit(col)

    def arrive(i, _):
        c = lax.rem(col + n_col - i, n_col)
        pltpu.make_async_remote_copy(
            src_ref=outgoing.at[0], dst_ref=incoming.at[c], send_sem=send_sem.at[c], recv_sem=recv_sem.at[c],
            device_id=(row, c), device_id_type=MESH,
        ).wait_recv()
        emit(c)
        return 0

    lax.fori_loop(1, n_col, arrive, 0)

    def sent(i, _):
        dcopy(lax.rem(col + i, n_col)).wait_send()
        return 0

    lax.fori_loop(1, n_col, sent, 0)
    for w, o in enumerate(others):
        rcopy(w, row, o).wait_send()

    @pl.when(col > 0)
    def _():
        down.wait_send()

    @pl.when(col < n_col - 1)
    def _():
        up.wait_send()


def on_device(n_row, n_col, a_blocks, block_rows, block_cols, block_count, restrict, interp, aggregate, owner):
    vmem = pl.BlockSpec(memory_space=pltpu.VMEM)
    smem = pl.BlockSpec(memory_space=pltpu.SMEM)
    width = n_col // (CORES * DEPTH)
    nb = restrict.shape[0]
    nj, piece = interp.shape[:2]
    slots = a_blocks.shape[2]
    agg_total = owner.shape[0]
    assert agg_total == n_col
    row_width = agg_total // n_row + 2
    col_width = 3
    limit = 40 * 2**20
    hbm = pl.BlockSpec(memory_space=pltpu.HBM)
    sized = jnp.transpose(a_blocks[0, 0], (1, 2, 0))
    rg, prod = pl.pallas_call(
        functools.partial(gather_kernel, n_row, n_col, 8),
        out_shape=(
            jax.ShapeDtypeStruct((n_col, nb, 32, 128), jnp.bfloat16),
            jax.ShapeDtypeStruct((slots, 32, 128), jnp.bfloat16),
        ),
        in_specs=[smem, hbm, hbm, hbm],
        out_specs=(vmem, vmem),
        scratch_shapes=[
            pltpu.VMEM((nb, 64, 64), jnp.bfloat16),
            pltpu.VMEM((nj, piece, 64), jnp.bfloat16),
            pltpu.VMEM((64, 64, slots), jnp.bfloat16),
            pltpu.VMEM((n_row, nj // 2, piece, 128), jnp.bfloat16),
            pltpu.VMEM((32 * slots, 128), jnp.float32),
            pltpu.VMEM((nj, 128, 128), jnp.bfloat16),
            pltpu.SemaphoreType.DMA((3,)),
            pltpu.SemaphoreType.DMA((n_col, 3 + width)),
            pltpu.SemaphoreType.DMA((n_col,)),
            pltpu.SemaphoreType.DMA((n_row,)),
            pltpu.SemaphoreType.DMA((n_row,)),
        ],
        compiler_params=pltpu.CompilerParams(collective_id=0, has_side_effects=True, vmem_limit_bytes=50_000_000),
        name="gather_panels",
    )(block_cols[0], restrict, interp, sized)
    part = pl.pallas_call(
        functools.partial(compute_kernel, n_row, n_col, row_width, col_width, 32),
        out_shape=jax.ShapeDtypeStruct((col_width, row_width, 32, 128), jnp.float32),
        in_specs=[smem, smem, smem, smem, vmem, vmem],
        out_specs=vmem,
        scratch_shapes=[pltpu.VMEM((row_width * col_width + 1, 32, 128), jnp.float32)],
        compiler_params=pltpu.CompilerParams(vmem_limit_bytes=24 * 2**20),
        name="local_terms",
    )(block_rows[0], block_cols[0], block_count, aggregate, prod, rg.reshape(n_col * nb, 32, 128))
    return pl.pallas_call(
        functools.partial(reduce_kernel, n_row, n_col, row_width),
        out_shape=jax.ShapeDtypeStruct((1, agg_total, 64, 64), jnp.float32),
        in_specs=[smem, vmem],
        out_specs=vmem,
        scratch_shapes=[
            pltpu.VMEM((2, row_width, 32, 128), jnp.bfloat16),
            pltpu.VMEM((2, row_width, 32, 128), jnp.bfloat16),
            pltpu.VMEM((n_row, row_width, 32, 128), jnp.bfloat16),
            pltpu.VMEM((n_col, 32, 128), jnp.bfloat16),
            pltpu.VMEM((n_col, 32, 128), jnp.bfloat16),
            pltpu.VMEM((n_col, 32, 128), jnp.bfloat16),
            pltpu.SMEM((n_col,), jnp.int32),
            pltpu.SemaphoreType.DMA((2,)),
            pltpu.SemaphoreType.DMA((2,)),
            pltpu.SemaphoreType.DMA((n_row,)),
            pltpu.SemaphoreType.DMA((n_row,)),
            pltpu.SemaphoreType.DMA((n_col,)),
            pltpu.SemaphoreType.DMA((n_col,)),
        ],
        compiler_params=pltpu.CompilerParams(collective_id=1, has_side_effects=True, vmem_limit_bytes=limit),
        name="reduce_coarse",
    )(owner, part)


def solution(mesh):
    return jax.shard_map(
        functools.partial(on_device, mesh.shape["row"], mesh.shape["col"]),
        mesh=mesh,
        in_specs=(
            P("row", "col", None, None, None),
            P("row", "col", None),
            P("row", "col", None),
            P("row", "col"),
            P(("row", "col"), None, None),
            P("col", "row", None),
            P(),
            P(),
        ),
        out_specs=P("col", None, None, None),
        check_vma=False,
    )
```

```python
import functools

import jax
import jax.numpy as jnp
from jax import lax
from jax.experimental import pallas as pl
from jax.experimental.pallas import tpu as pltpu
from jax.sharding import PartitionSpec as P

MESH = pl.DeviceIdType.MESH
CORES = 2
DEPTH = 4


def gather_kernel(n_row, n_col, unroll, cols_ref, r_hbm, p_hbm, a_hbm, rg_ref, prod_ref, r_ref, p_ref, a_ref, pg_ref, flat, wide, load_sem, send_sem, recv_sem, psend_sem, precv_sem):
    width = n_col // (CORES * DEPTH)
    me = lax.axis_index("col")
    row = lax.axis_index("row")
    z = me // (width * CORES)
    x = lax.rem(me // CORES, width)
    k = lax.rem(me, CORES)
    sibling = me + 1 - 2 * k
    hop = width * CORES
    other_x = [(z * width + lax.rem(x + d, width)) * CORES + k for d in range(1, width)]
    other_row = [lax.rem(row + d, n_row) for d in range(1, n_row)]
    nb = r_ref.shape[0]
    half_p = p_ref.shape[0] // 2
    piece = p_ref.shape[1]
    slots = a_ref.shape[2]

    load_r = pltpu.make_async_copy(r_hbm, r_ref, load_sem.at[0])
    load_p = pltpu.make_async_copy(p_hbm, p_ref, load_sem.at[1])
    load_a = pltpu.make_async_copy(a_hbm, a_ref, load_sem.at[2])
    load_r.start()
    load_p.start()
    load_a.start()

    barrier = pltpu.get_barrier_semaphore()

    def greet(dev):
        pl.semaphore_signal(barrier, inc=1, device_id=dev, device_id_type=MESH)

    for o in other_row:
        greet((o, me))
    greet((row, sibling))
    for o in other_x:
        greet((row, o))

    @pl.when(z > 0)
    def _():
        greet((row, me - hop))

    @pl.when(z < DEPTH - 1)
    def _():
        greet((row, me + hop))

    load_r.wait()
    for i in range(nb):
        rg_ref[me, i, :, 0:64] = r_ref[i, 0:32]
        rg_ref[me, i, :, 64:128] = r_ref[i, 32:64]
    load_p.wait()
    for j in range(half_p):
        pg_ref[row, j, :, 0:64] = p_ref[j]
        pg_ref[row, j, :, 64:128] = p_ref[j + half_p]

    fixed = len(other_row) + 1 + len(other_x)
    pl.semaphore_wait(barrier, fixed + jnp.where(z > 0, 1, 0) + jnp.where(z < DEPTH - 1, 1, 0))

    def rcopy(shard, way, target):
        return pltpu.make_async_remote_copy(
            src_ref=rg_ref.at[shard],
            dst_ref=rg_ref.at[shard],
            send_sem=send_sem.at[shard, way],
            recv_sem=recv_sem.at[shard],
            device_id=(row, target),
            device_id_type=MESH,
        )

    def pcopy(way, target):
        return pltpu.make_async_remote_copy(
            src_ref=pg_ref.at[row],
            dst_ref=pg_ref.at[row],
            send_sem=psend_sem.at[way],
            recv_sem=precv_sem.at[row],
            device_id=(target, me),
            device_id_type=MESH,
        )

    def spread(shard):
        for w, o in enumerate(other_x):
            rcopy(shard, 3 + w, o).start()
        rcopy(shard, 0, sibling).start()

    @pl.when(z > 0)
    def _():
        rcopy(me, 1, me - hop).start()

    @pl.when(z < DEPTH - 1)
    def _():
        rcopy(me, 2, me + hop).start()

    for w, o in enumerate(other_row):
        pcopy(w, o).start()
    spread(me)

    def from_z(d):
        @pl.when(z - d >= 0)
        def _():
            shard = me - d * hop
            rcopy(shard, 0, sibling).wait_recv()

            @pl.when(z < DEPTH - 1)
            def _():
                rcopy(shard, 2, me + hop).start()

            spread(shard)

        @pl.when(z + d < DEPTH)
        def _():
            shard = me + d * hop
            rcopy(shard, 0, sibling).wait_recv()

            @pl.when(z > 0)
            def _():
                rcopy(shard, 1, me - hop).start()

            spread(shard)

    def from_x(d):
        for sign in ((1,) if d == 0 else (-1, 1)):
            @pl.when((z + sign * d >= 0) & (z + sign * d < DEPTH))
            def _():
                for o in other_x:
                    shard = o + sign * d * hop
                    rcopy(shard, 0, sibling).wait_recv()
                    rcopy(shard, 0, sibling).start()

    def turn(lo, hi):
        def body(i, _):
            for s in range(0, slots, 128):
                e = min(s + 128, slots)
                tall = jnp.concatenate([a_ref[i, :, s:e], a_ref[i + 32, :, s:e]], axis=0)
                flat[pl.ds(pl.multiple_of(i * slots + s, 8), e - s), :] = tall.astype(jnp.float32).T
            return 0

        lax.fori_loop(lo, hi, body, 0)

    def multiply(lo, hi):
        def body(g, _):
            base = g * unroll
            made = []
            for u in range(unroll):
                left = flat[pl.ds(base + u, 32, stride=slots), :].astype(jnp.bfloat16)
                made.append(
                    jnp.dot(left, wide[cols_ref[0, base + u]], preferred_element_type=jnp.float32).astype(jnp.bfloat16)
                )
            for u in range(unroll):
                prod_ref[base + u] = made[u]
            return 0

        lax.fori_loop(lo, hi, body, 0)

    def widen(j, _):
        for r in range(n_row):
            lo, hi = r * piece, (r + 1) * piece
            both = pg_ref[r, j]
            wide[j, lo:hi, 0:64] = both[:, 0:64]
            wide[j, 64 + lo:64 + hi, 64:128] = both[:, 0:64]
            wide[j + half_p, lo:hi, 0:64] = both[:, 64:128]
            wide[j + half_p, 64 + lo:64 + hi, 64:128] = both[:, 64:128]
        return 0

    load_a.wait()
    turn(0, 12)
    from_z(1)
    turn(12, 22)
    from_x(0)
    turn(22, 32)
    from_z(2)
    for o in other_row:
        pltpu.make_async_remote_copy(
            src_ref=pg_ref.at[o], dst_ref=pg_ref.at[o], send_sem=psend_sem.at[0], recv_sem=precv_sem.at[o],
            device_id=(o, me), device_id_type=MESH,
        ).wait_recv()
    wide[...] = jnp.zeros_like(wide)
    lax.fori_loop(0, half_p, widen, 0, unroll=2)
    from_x(1)
    groups = slots // unroll
    multiply(0, groups // 4)
    from_z(3)
    multiply(groups // 4, groups // 2)
    from_x(2)
    multiply(groups // 2, 3 * groups // 4)
    from_x(3)
    multiply(3 * groups // 4, groups)

    for other in range(n_col // CORES):
        rcopy(other * CORES + 1 - k, 0, sibling).wait_recv()
    for other in range(n_col // CORES):
        rcopy(other * CORES + k, 0, sibling).wait_send()
    for zz in range(DEPTH):
        shard = (zz * width + x) * CORES + k
        for w in range(len(other_x)):
            rcopy(shard, 3 + w, me).wait_send()

        @pl.when((z > 0) & (zz >= z))
        def _():
            rcopy(shard, 1, me).wait_send()

        @pl.when((z < DEPTH - 1) & (zz <= z))
        def _():
            rcopy(shard, 2, me).wait_send()
    for w in range(len(other_row)):
        pcopy(w, row).wait_send()


def compute_kernel(n_row, n_col, row_width, col_width, unroll, rows_ref, cols_ref, count_ref, agg_ref, prod_ref, r_full, out_ref, acc):
    row = lax.axis_index("row")
    col = lax.axis_index("col")
    panel_rows = r_full.shape[0]
    panel_cols = agg_ref.shape[0] // n_col
    n_seg = row_width * col_width
    agg_total = n_col
    row_base = row * (agg_total // n_row) - 1
    col_base = col - 1

    acc[...] = jnp.zeros_like(acc)
    count = count_ref[0, 0]
    left_half = lax.broadcasted_iota(jnp.int32, (32, 128), 1) < 64
    none = jnp.zeros((32, 128), jnp.bfloat16)

    def group(g, _):
        base = g * unroll
        terms = []
        for u in range(unroll):
            both = prod_ref[base + u]
            turned = jnp.concatenate([both[:, 64:128], both[:, 0:64]], axis=1)
            right = jnp.concatenate(
                [
                    jnp.where(left_half, both, none),
                    jnp.where(left_half, turned, none),
                    jnp.where(left_half, none, turned),
                    jnp.where(left_half, none, both),
                ],
                axis=0,
            )
            terms.append(jnp.dot(r_full[rows_ref[0, base + u]], right, preferred_element_type=jnp.float32))
        for u in range(unroll):
            p = base + u
            ra = agg_ref[row * panel_rows + rows_ref[0, p]] - row_base
            ca = agg_ref[col * panel_cols + cols_ref[0, p]] - col_base
            seg = jnp.where(p < count, ra * col_width + ca, n_seg)
            acc[seg] += terms[u]
        return 0

    lax.fori_loop(0, pl.cdiv(count, unroll), group, 0)
    for ca in range(col_width):
        for ra in range(row_width):
            out_ref[ca, ra] = acc[ra * col_width + ca]


def reduce_kernel(n_row, n_col, row_width, owner_ref, part_ref, out_ref, away, edge, rows_in, outgoing, incoming, full, inverse, esend_sem, erecv_sem, rsend_sem, rrecv_sem, send_sem, recv_sem):
    row = lax.axis_index("row")
    col = lax.axis_index("col")
    panel_agg = n_col // n_row
    others = [lax.rem(row + d, n_row) for d in range(1, n_row)]

    barrier = pltpu.get_barrier_semaphore()

    def greet(i, _):
        pl.semaphore_signal(barrier, inc=1, device_id=(row, lax.rem(col + i, n_col)), device_id_type=MESH)
        return 0

    lax.fori_loop(1, n_col, greet, 0)
    for o in others:
        pl.semaphore_signal(barrier, inc=1, device_id=(o, col), device_id_type=MESH)
    away[0] = part_ref[0].astype(jnp.bfloat16)
    away[1] = part_ref[2].astype(jnp.bfloat16)
    pl.semaphore_wait(barrier, n_col - 1 + len(others))

    def ecopy(side, target):
        return pltpu.make_async_remote_copy(
            src_ref=away.at[side], dst_ref=edge.at[side], send_sem=esend_sem.at[side], recv_sem=erecv_sem.at[side],
            device_id=(row, target), device_id_type=MESH,
        )

    down = ecopy(0, col - 1)
    up = ecopy(1, col + 1)

    @pl.when(col > 0)
    def _():
        down.start()

    @pl.when(col < n_col - 1)
    def _():
        up.start()

    def invert(s, _):
        inverse[s] = lax.fori_loop(0, n_col, lambda t, got: jnp.where(owner_ref[t] == s, t, got), 0, unroll=True)
        return 0

    lax.fori_loop(0, n_col, invert, 0)

    @pl.when(col == 0)
    def _():
        edge[1] = jnp.zeros_like(edge[1])

    @pl.when(col == n_col - 1)
    def _():
        edge[0] = jnp.zeros_like(edge[0])

    @pl.when(col > 0)
    def _():
        up.wait_recv()

    @pl.when(col < n_col - 1)
    def _():
        down.wait_recv()

    rows_in[row] = (part_ref[1] + edge[0].astype(jnp.float32) + edge[1].astype(jnp.float32)).astype(jnp.bfloat16)

    def rcopy(way, source, target):
        return pltpu.make_async_remote_copy(
            src_ref=rows_in.at[source], dst_ref=rows_in.at[source], send_sem=rsend_sem.at[way], recv_sem=rrecv_sem.at[source],
            device_id=(target, col), device_id_type=MESH,
        )

    for w, o in enumerate(others):
        rcopy(w, row, o).start()
    for o in others:
        rcopy(0, o, o).wait_recv()
    for a in range(n_col):
        pieces = [
            rows_in[r, a - r * panel_agg + 1].astype(jnp.float32)
            for r in range(n_row)
            if 0 <= a - r * panel_agg + 1 < row_width
        ]
        full[a] = functools.reduce(jnp.add, pieces).astype(jnp.bfloat16)

    def dcopy(s):
        return pltpu.make_async_remote_copy(
            src_ref=outgoing.at[s], dst_ref=incoming.at[col], send_sem=send_sem.at[s], recv_sem=recv_sem.at[col],
            device_id=(row, s), device_id_type=MESH,
        )

    def post(i, _):
        s = lax.rem(col + i, n_col)
        outgoing[s] = full[inverse[s]]
        dcopy(s).start()
        return 0

    lax.fori_loop(1, n_col, post, 0)
    incoming[col] = full[inverse[col]]

    def emit(c):
        block = incoming[c].astype(jnp.float32)
        out_ref[0, c, 0:32, :] = block[:, 0:64]
        out_ref[0, c, 32:64, :] = block[:, 64:128]

    emit(col)

    def arrive(i, _):
        c = lax.rem(col + n_col - i, n_col)
        pltpu.make_async_remote_copy(
            src_ref=outgoing.at[0], dst_ref=incoming.at[c], send_sem=send_sem.at[c], recv_sem=recv_sem.at[c],
            device_id=(row, c), device_id_type=MESH,
        ).wait_recv()
        emit(c)
        return 0

    lax.fori_loop(1, n_col, arrive, 0)

    def sent(i, _):
        dcopy(lax.rem(col + i, n_col)).wait_send()
        return 0

    lax.fori_loop(1, n_col, sent, 0)
    for w, o in enumerate(others):
        rcopy(w, row, o).wait_send()

    @pl.when(col > 0)
    def _():
        down.wait_send()

    @pl.when(col < n_col - 1)
    def _():
        up.wait_send()


def on_device(n_row, n_col, a_blocks, block_rows, block_cols, block_count, restrict, interp, aggregate, owner):
    vmem = pl.BlockSpec(memory_space=pltpu.VMEM)
    smem = pl.BlockSpec(memory_space=pltpu.SMEM)
    width = n_col // (CORES * DEPTH)
    nb = restrict.shape[0]
    nj, piece = interp.shape[:2]
    slots = a_blocks.shape[2]
    agg_total = owner.shape[0]
    assert agg_total == n_col
    row_width = agg_total // n_row + 2
    col_width = 3
    limit = 40 * 2**20
    hbm = pl.BlockSpec(memory_space=pltpu.HBM)
    sized = jnp.transpose(a_blocks[0, 0], (1, 2, 0))
    rg, prod = pl.pallas_call(
        functools.partial(gather_kernel, n_row, n_col, 32),
        out_shape=(
            jax.ShapeDtypeStruct((n_col, nb, 32, 128), jnp.bfloat16),
            jax.ShapeDtypeStruct((slots, 32, 128), jnp.bfloat16),
        ),
        in_specs=[smem, hbm, hbm, hbm],
        out_specs=(vmem, vmem),
        scratch_shapes=[
            pltpu.VMEM((nb, 64, 64), jnp.bfloat16),
            pltpu.VMEM((nj, piece, 64), jnp.bfloat16),
            pltpu.VMEM((64, 64, slots), jnp.bfloat16),
            pltpu.VMEM((n_row, nj // 2, piece, 128), jnp.bfloat16),
            pltpu.VMEM((32 * slots, 128), jnp.float32),
            pltpu.VMEM((nj, 128, 128), jnp.bfloat16),
            pltpu.SemaphoreType.DMA((3,)),
            pltpu.SemaphoreType.DMA((n_col, 3 + width)),
            pltpu.SemaphoreType.DMA((n_col,)),
            pltpu.SemaphoreType.DMA((n_row,)),
            pltpu.SemaphoreType.DMA((n_row,)),
        ],
        compiler_params=pltpu.CompilerParams(collective_id=0, has_side_effects=True, vmem_limit_bytes=50_000_000),
        name="gather_panels",
    )(block_cols[0], restrict, interp, sized)
    part = pl.pallas_call(
        functools.partial(compute_kernel, n_row, n_col, row_width, col_width, 32),
        out_shape=jax.ShapeDtypeStruct((col_width, row_width, 32, 128), jnp.float32),
        in_specs=[smem, smem, smem, smem, vmem, vmem],
        out_specs=vmem,
        scratch_shapes=[pltpu.VMEM((row_width * col_width + 1, 32, 128), jnp.float32)],
        compiler_params=pltpu.CompilerParams(vmem_limit_bytes=24 * 2**20),
        name="local_terms",
    )(block_rows[0], block_cols[0], block_count, aggregate, prod, rg.reshape(n_col * nb, 32, 128))
    return pl.pallas_call(
        functools.partial(reduce_kernel, n_row, n_col, row_width),
        out_shape=jax.ShapeDtypeStruct((1, agg_total, 64, 64), jnp.float32),
        in_specs=[smem, vmem],
        out_specs=vmem,
        scratch_shapes=[
            pltpu.VMEM((2, row_width, 32, 128), jnp.bfloat16),
            pltpu.VMEM((2, row_width, 32, 128), jnp.bfloat16),
            pltpu.VMEM((n_row, row_width, 32, 128), jnp.bfloat16),
            pltpu.VMEM((n_col, 32, 128), jnp.bfloat16),
            pltpu.VMEM((n_col, 32, 128), jnp.bfloat16),
            pltpu.VMEM((n_col, 32, 128), jnp.bfloat16),
            pltpu.SMEM((n_col,), jnp.int32),
            pltpu.SemaphoreType.DMA((2,)),
            pltpu.SemaphoreType.DMA((2,)),
            pltpu.SemaphoreType.DMA((n_row,)),
            pltpu.SemaphoreType.DMA((n_row,)),
            pltpu.SemaphoreType.DMA((n_col,)),
            pltpu.SemaphoreType.DMA((n_col,)),
        ],
        compiler_params=pltpu.CompilerParams(collective_id=1, has_side_effects=True, vmem_limit_bytes=limit),
        name="reduce_coarse",
    )(owner, part)


def solution(mesh):
    return jax.shard_map(
        functools.partial(on_device, mesh.shape["row"], mesh.shape["col"]),
        mesh=mesh,
        in_specs=(
            P("row", "col", None, None, None),
            P("row", "col", None),
            P("row", "col", None),
            P("row", "col"),
            P(("row", "col"), None, None),
            P("col", "row", None),
            P(),
            P(),
        ),
        out_specs=P("col", None, None, None),
        check_vma=False,
    )
```
